256 devices in a mesh: tile: 32 (over z, x), mem: 8 (over y, core).
Axes of the slice: x: 4, y: 4, z: 8, core: 2. Of those that a mesh axis runs over, the one named last changes fastest.
Arguments:
- ensemble: bfloat16 [64, 512, 1024], P('mem', 'tile'), may hold values from -8 to 8
- obs_members: bfloat16 [32768, 64, 128], P(('tile', 'mem')), may hold values from -6 to 6
- obs_values: float32 [32768, 128], P(('tile', 'mem')), may hold values from -9 to 9
- obs_weight: float32 [32768, 128], P(('tile', 'mem')), may hold values from 0.05 to 1
- obs_count: int32 [32768], P(('tile', 'mem')), may hold values from 1 to 128
- obs_tile: int32 [32768], P(('tile', 'mem')), may hold values from 0 to 31, as said below
- obs_block: int32 [32768], P(('tile', 'mem')), may hold values from 0 to 15
- obs_turn: int32 [32768], P(('tile', 'mem')), may hold values from 0 to 3
Outputs:
- analysis_pert: bfloat16 [64, 512, 1024], P('mem', 'tile')
- analysis_mean: bfloat16 [512, 1024], P(('tile', 'mem'))
The draws below stay inside these ranges and needn't reach their ends.
Inputs may be any that keep to these rules, and one draw needn't show every extreme that they name: `obs_tile`: within each aligned group of 128 consecutive blocks (the blocks of one device), no tile is named more than 8 times, and one tile is named exactly 8 times by every group.
All inputs are finite; a program needn't handle non-finite values.
Results may differ from the reference program's by a relative error of at most 0.0036.
Values may be sent and summed in bfloat16 or wider, within the bound.
A program may use at most 64 MiB of HBM per device.

```python
import math
import jax
import jax.numpy as jnp
from jax import lax

MEMBERS = 64
BPS = 4
ROWS = 128
OBD = 128
NS_STEPS = 6
ABLK = 16
LEVBC = 1024
NBLK = 512
NOB = 32768
N_TILE = 32


def draw_ensemble(key, part):
    centre_key = jax.random.fold_in(key, 11)
    member_key = jax.random.fold_in(key, 12)
    centre = jax.random.normal(centre_key, (NBLK, LEVBC), jnp.float32)
    members = 0.7 * jax.random.normal(member_key, (MEMBERS, NBLK, LEVBC), jnp.float32)
    return jnp.clip(centre[None] + members, -8.0, 8.0).astype(jnp.bfloat16)


def draw_obs_tile(key, part):
    capacity = max(2, 2 * OBD // N_TILE)
    slot_count = N_TILE * capacity
    liking = jax.random.randint(jax.random.fold_in(key, 21), (N_TILE,), 0, 4)
    hottest = jax.random.randint(jax.random.fold_in(key, 22), (), 0, N_TILE)
    slot_tile = jnp.arange(slot_count, dtype=jnp.int32) // capacity
    favour = liking[slot_tile] * 32768 + jnp.where(slot_tile == hottest, 1048576, 0)

    def one_source(source):
        source_key = jax.random.fold_in(jax.random.fold_in(key, 23), source)
        jitter = jax.random.randint(source_key, (slot_count,), 0, 65536)
        scores = (jitter + favour) * slot_count + jnp.arange(slot_count, dtype=jnp.int32)
        _, picked = lax.top_k(scores, OBD)
        shuffle = jax.random.permutation(jax.random.fold_in(source_key, 1), OBD)
        return (picked // capacity)[shuffle].astype(jnp.int32)
    sources = jnp.arange(NOB // OBD, dtype=jnp.int32)
    return jax.vmap(one_source)(sources).reshape(NOB)


def with_ends(array, rng, low, largest):
    shape = array.shape
    spot = [jax.random.randint(jax.random.fold_in(rng, axis), (), 0, shape[axis]) for axis in range(len(shape))]
    array = array.at[tuple(spot)].set(low)
    longest = shape.index(max(shape))
    spot[longest] = (spot[longest] + 1) % shape[longest]
    return array.at[tuple(spot)].set(largest)


def block_levels(stream_key, dims, cuts, least, high):
    def one(dim, shards_of):
        steps = jax.random.uniform(jax.random.fold_in(jax.random.fold_in(stream_key, 6), dim), (shards_of,), jnp.float32, least / len(cuts), high / len(cuts))
        return jnp.repeat(jnp.exp(steps), dims[dim] // shards_of).reshape((-1,) + (1,) * (len(dims) - dim - 1))

    loudness = one(*cuts[0])
    for cut in cuts[1:]:
        loudness = loudness * one(*cut)
    return loudness


def bell_draw(key, extent, scale, limit, shards=(), held_as=jnp.bfloat16):
    values = scale * jax.random.normal(key, extent, jnp.float32)
    if shards:
        values = values * block_levels(key, extent, shards, -0.22, 0.18)
    return jnp.clip(values, -limit, limit).astype(held_as)


def setup_inputs(seed: int = 0) -> dict:
    keys = jax.random.split(jax.random.key(seed), 9)
    ensemble = draw_ensemble(jax.random.fold_in(keys[8], 71), 0)
    obs_members = bell_draw(keys[1], (NOB, MEMBERS, ROWS), 1.0, 6.0, ((0, 256),))
    obs_values = bell_draw(keys[2], (NOB, ROWS), 1.5, 9.0, ((0, 256),), jnp.float32)
    obs_weight = jnp.clip(jnp.exp(math.log(1.0) - 2.9957323 * jax.random.uniform(keys[3], (NOB, ROWS), jnp.float32) ** block_levels(keys[3], (NOB, ROWS), ((0, 256),), -0.2, 0.2)), 0.05, 1.0)
    obs_count = with_ends(jax.random.randint(keys[4], (NOB,), 1, ROWS + 1), jax.random.fold_in(keys[4], 1), 1, ROWS).astype(jnp.int32)
    obs_tile = draw_obs_tile(jax.random.fold_in(keys[8], 71), 0)
    obs_block = with_ends(jax.random.randint(keys[6], (NOB,), 0, ABLK), jax.random.fold_in(keys[6], 1), 0, ABLK - 1).astype(jnp.int32)
    obs_turn = with_ends(jax.random.randint(keys[7], (NOB,), 0, 4), jax.random.fold_in(keys[7], 1), 0, 3).astype(jnp.int32)
    return {"ensemble": ensemble, "obs_members": obs_members, "obs_values": obs_values, "obs_weight": obs_weight, "obs_count": obs_count, "obs_tile": obs_tile, "obs_block": obs_block, "obs_turn": obs_turn}


def product(left, right):
    return jnp.matmul(left, right, precision=lax.Precision.HIGHEST)

def target_block(obs_block, obs_turn):
    block_row = obs_block // BPS
    block_col = obs_block % BPS
    last = BPS - 1
    new_row = jnp.where(obs_turn == 0, block_row, jnp.where(obs_turn == 1, block_col, jnp.where(obs_turn == 2, last - block_row, last - block_col)))
    new_col = jnp.where(obs_turn == 0, block_col, jnp.where(obs_turn == 1, last - block_row, jnp.where(obs_turn == 2, last - block_col, block_row)))
    return (new_row * BPS + new_col).astype(jnp.int32)

def scaled_obs(obs_members, obs_values, obs_weight, obs_count):
    obs_mean = lax.optimization_barrier(jnp.sum(obs_members.astype(jnp.float32), axis=1)) / MEMBERS
    usable = lax.broadcasted_iota(jnp.int32, obs_weight.shape, 1) < obs_count[:, None]
    weight_root = jnp.sqrt(jnp.where(usable, obs_weight, jnp.zeros_like(obs_weight)))
    scaled_pert = ((obs_members.astype(jnp.float32) - obs_mean[:, None, :]) * weight_root[:, None, :]).astype(jnp.bfloat16)
    scaled_innov = ((obs_values - obs_mean) * weight_root).astype(jnp.bfloat16)
    return (scaled_pert, scaled_innov)

def transforms(gram, projection):
    identity = jnp.eye(MEMBERS, dtype=jnp.float32)
    system = (MEMBERS - 1.0) * identity + gram
    frob = jnp.sqrt(lax.optimization_barrier(jnp.sum(system * system, axis=(1, 2))))[:, None, None]
    square_root = system / frob
    inverse = jnp.broadcast_to(identity, system.shape)
    for sweep in range(NS_STEPS):
        middle = 1.5 * identity - 0.5 * product(inverse, square_root)
        square_root = product(square_root, middle)
        inverse = product(middle, inverse)
    inverse_root = inverse / jnp.sqrt(frob)
    covariance = product(inverse_root, inverse_root)
    mean_weights = jnp.einsum('bjk,bk->bj', covariance, projection, precision=lax.Precision.HIGHEST).astype(jnp.bfloat16)
    spread = (jnp.sqrt(MEMBERS - 1.0) * inverse_root).astype(jnp.bfloat16)
    return (spread, mean_weights)

def reference(ensemble, obs_members, obs_values, obs_weight, obs_count, obs_tile, obs_block, obs_turn):
    scaled_pert, scaled_innov = scaled_obs(obs_members, obs_values, obs_weight, obs_count)
    segment = (obs_tile * ABLK + target_block(obs_block, obs_turn)).astype(jnp.int32)
    groups = NOB // OBD

    def add_group(carry, pieces):
        gram_total, proj_total = carry
        pert_piece, innov_piece, seg_piece = pieces
        pert_float = pert_piece.astype(jnp.float32)
        innov_float = innov_piece.astype(jnp.float32)
        grams = jnp.einsum('nkr,nlr->nkl', pert_float, pert_float, precision=lax.Precision.HIGHEST)
        projs = jnp.einsum('nkr,nr->nk', pert_float, innov_float, precision=lax.Precision.HIGHEST)
        return ((gram_total.at[seg_piece].add(grams), proj_total.at[seg_piece].add(projs)), None)
    start = (jnp.zeros((NBLK, MEMBERS, MEMBERS), jnp.float32), jnp.zeros((NBLK, MEMBERS), jnp.float32))
    pieces = (scaled_pert.reshape(groups, OBD, MEMBERS, ROWS), scaled_innov.reshape(groups, OBD, ROWS), segment.reshape(groups, OBD))
    (gram, projection), _ = lax.scan(add_group, start, pieces)
    spread, mean_weights = transforms(gram, projection)
    background_mean = lax.optimization_barrier(jnp.sum(ensemble.astype(jnp.float32), axis=0)) / MEMBERS
    perturbation = (ensemble.astype(jnp.float32) - background_mean[None]).astype(jnp.bfloat16)
    pert_float = perturbation.astype(jnp.float32)
    analysis_pert = jnp.einsum('jbx,bjk->kbx', pert_float, spread.astype(jnp.float32), precision=lax.Precision.HIGHEST).astype(jnp.bfloat16)
    increment = jnp.einsum('jbx,bj->bx', pert_float, mean_weights.astype(jnp.float32), precision=lax.Precision.HIGHEST)
    analysis_mean = (background_mean + increment).astype(jnp.bfloat16)
    return (analysis_pert, analysis_mean)
```

```python
import functools

import jax
import jax.numpy as jnp
from jax import lax
from jax.experimental import pallas as pl
from jax.experimental.pallas import tpu as pltpu
from jax.sharding import PartitionSpec as P

MESH = pl.DeviceIdType.MESH
MEMBERS = 64
ROWS = 128
OBD = 128
NS_STEPS = 6
NX, NY, NZ = 4, 4, 8
PACKED = 17
F32, BF16 = jnp.float32, jnp.bfloat16
CHUNKS = 8


def iota(shape, dim):
    return lax.broadcasted_iota(jnp.int32, shape, dim)


def nt(left, right):
    return lax.dot_general(left, right, (((1,), (1,)), ((), ())), preferred_element_type=F32)


def split(value):
    high = value.astype(BF16)
    return high, (value - high.astype(F32)).astype(BF16)


def product(left, right):
    (lh, ll), (rh, rl) = split(left), split(right)
    dot = functools.partial(jnp.dot, preferred_element_type=F32)
    return dot(lh, rh) + (dot(lh, rl) + dot(ll, rh))


def cell_rows(tile, block, turn, z, x, y, c):
    row, col = block // 4, block % 4
    new_row = jnp.where(turn == 0, row, jnp.where(turn == 1, col, jnp.where(turn == 2, 3 - row, 3 - col)))
    new_col = jnp.where(turn == 0, col, jnp.where(turn == 1, 3 - row, jnp.where(turn == 2, 3 - col, row)))
    dy = (new_row + NY - y) & 3
    dc = (new_col // 2 + c) & 1
    half = new_col & 1
    dz = ((tile // 4) + NZ - z) & 7
    dx = ((tile & 3) + NX - x) & 3
    inner = jnp.where(half == 0, dy * 32 + dx * 8, dx * 32 + dy * 8) + dz
    return dc * 256 + half * 128 + inner


def transforms(packed):
    main, extra = packed[:16], packed[16:17]
    lane, sub = iota((16, 128), 1), iota((16, 128), 0)
    col = lane & 15
    back = pltpu.roll(main, 112, 1)
    far = pltpu.roll(main, 64, 1)
    far_back = pltpu.roll(back, 64, 1)
    zero = jnp.zeros_like(main)
    row_d = jnp.where((lane < 48) | ((lane < 64) & (col < sub)), main, zero)
    row_c = jnp.where(lane < 32, far, jnp.where((lane < 48) & (col > sub), back, zero))
    ba = pltpu.roll(main, 32, 1)
    row_b = jnp.where((lane < 16) | ((lane < 32) & (col < sub)), ba, zero)
    aa = pltpu.roll(main, 16, 1)
    row_a = jnp.where((lane < 16) & (col > sub), aa, zero)
    del far_back
    half = jnp.concatenate([row_a, row_b, row_c, row_d], axis=0)
    full = jnp.concatenate([half, jnp.zeros((64, 128), F32)], axis=0)
    both = (full + full.T)[:64, :64]
    diag = pltpu.roll(jnp.broadcast_to(extra, (8, 128)), 64, 1)[0:1, :64]
    eye = iota((64, 64), 0) == iota((64, 64), 1)
    system = both + jnp.where(eye, diag + (MEMBERS - 1.0), 0.0)
    frob = jnp.sqrt(jnp.sum(system * system, axis=(0, 1), keepdims=True))
    root = system / frob
    identity = jnp.where(eye, 1.0, 0.0)
    middle = 1.5 * identity - 0.5 * root
    inverse = middle
    root = product(root, middle)
    for sweep in range(1, NS_STEPS):
        middle = 1.5 * identity - 0.5 * product(inverse, root)
        if sweep < NS_STEPS - 1:
            root = product(root, middle)
        inverse = product(middle, inverse)
    inverse_root = inverse / jnp.sqrt(frob)
    projection = jnp.broadcast_to(extra[:, :64], (16, 64))
    weights = product(product(projection, inverse_root), inverse_root)
    spread = (jnp.sqrt(F32(MEMBERS - 1.0)) * inverse_root).astype(BF16)
    return jnp.concatenate([spread, weights.astype(BF16)], axis=0)


def kernel(
    ens_ref, members_ref, values_ref, weight_ref, count_ref, tile_ref, block_ref, turn_ref,
    out_ref, mean_ref,
    obs, ens_f, ens_s, ens_r, pert_s, root_s, flat, core_s, core_r, own, s1, r1, acc1, s2, r2, acc2,
    s3, r3, ana,
    load_sem, ens_ss, ens_rs, core_ss, core_rs, ss1, rs1, ss2, rs2, ss3, rs3, out_ss, out_rs, self_sem,
):
    t, m = lax.axis_index("tile"), lax.axis_index("mem")
    z, x, y, c = t // 4, t % 4, m // 2, m % 2

    def at_mem(step):
        return (t, lax.rem(m + step, 8))

    def at_core():
        return (t, y * 2 + 1 - c)

    def at_y(step):
        return (t, lax.rem(y + step, NY) * 2 + c)

    def at_x(step):
        return (z * 4 + lax.rem(x + step, NX), m)

    def at_z(step):
        return (lax.rem(z + step, NZ) * 4 + x, m)

    def remote(src, dst, send_sem, recv_sem, device):
        return pltpu.make_async_remote_copy(
            src_ref=src, dst_ref=dst, send_sem=send_sem, recv_sem=recv_sem, device_id=device, device_id_type=MESH
        )

    barrier = pltpu.get_barrier_semaphore()
    partners = [at_mem(s) for s in range(1, 8)] + [at_x(s) for s in range(1, NX)] + [at_z(s) for s in range(1, NZ)]
    for device in partners:
        pl.semaphore_signal(barrier, inc=1, device_id=device, device_id_type=MESH)

    per = OBD // CHUNKS
    loads = [
        pltpu.make_async_copy(members_ref.at[pl.ds(i * per, per)], obs.at[pl.ds(i * per, per)], load_sem.at[i])
        for i in range(CHUNKS)
    ]
    for load in loads:
        load.start()

    for j in range(8):
        for k in range(8):
            ens_f[j, pl.ds(k, 16, stride=8), :] = ens_ref[k, :, j * 128 : j * 128 + 128].astype(F32)
        ens_s[:, :, :, j * 128 : j * 128 + 128] = ens_f[j].reshape(8, 2, 8, 128).astype(BF16)

    pl.semaphore_wait(barrier, len(partners))
    ens_copies = [
        remote(ens_s.at[lax.rem(m + s, 8)], ens_r.at[m], ens_ss.at[s], ens_rs.at[s], at_mem(s)) for s in range(1, 8)
    ]
    for copy in ens_copies:
        copy.start()

    count = jnp.broadcast_to(count_ref[...].astype(F32), (OBD, OBD)).T
    usable = iota((OBD, ROWS), 1).astype(F32) < count
    root_s[...] = jnp.sqrt(jnp.where(usable, weight_ref[...], 0.0))

    lane, sub = iota((16, 128), 1), iota((16, 128), 0)
    col = lane & 15
    rolled_in = ((lane & 63) >= 48) & (col > sub)
    on_diag = (lane < 64) & (col == sub)

    def one_block(n):
        raw = obs[n].astype(F32)
        mean = jnp.sum(raw, axis=0, keepdims=True) / MEMBERS
        scale = root_s[pl.ds(n, 1), :]
        pert = ((raw - mean) * scale).astype(BF16)
        innov = ((values_ref[pl.ds(n, 1), :] - mean) * scale).astype(BF16)
        left = jnp.concatenate([pert, jnp.broadcast_to(innov, (16, ROWS))], axis=0)
        right = jnp.concatenate([pert, pert[:32], pert[:32]], axis=0)
        gram = nt(left, right)
        a, b, cc, d, p = gram[:16], gram[16:32], gram[32:48], gram[48:64], gram[64:65]
        rolled = pltpu.roll(jnp.where(lane < 64, cc, a), 16, 1)
        base = jnp.where(lane < 64, d, jnp.where(lane < 96, cc, b))
        flat[pl.ds(n, 16, stride=OBD), :] = jnp.where(rolled_in, rolled, base)
        four = jnp.where(lane < 16, a, jnp.where(lane < 32, b, jnp.where(lane < 48, cc, d)))
        diag = jnp.sum(jnp.where(on_diag, four, 0.0), axis=0, keepdims=True)
        flat[pl.ds(16 * OBD + n, 1), :] = jnp.where(lane[:1] < 64, p, pltpu.roll(diag, 64, 1))

    for i in range(CHUNKS):
        loads[i].wait()

        def two_blocks(n, carry, i=i):
            for u in range(4):
                one_block(i * per + n * 4 + u)
            return carry

        lax.fori_loop(0, per // 4, two_blocks, 0)

    rows = cell_rows(tile_ref[...], block_ref[...], turn_ref[...], z, x, y, c)
    ids = iota((256, OBD), 0)
    for_other = jnp.where(ids + 256 == rows, 1.0, 0.0).astype(BF16)
    for_self = jnp.where(ids == rows, 1.0, 0.0).astype(BF16)

    def to_cells(hot, keep):
        def pair(k, carry):
            at = pl.multiple_of(k * 256, 256)
            data = jnp.concatenate([flat[pl.ds(at, OBD), :], flat[pl.ds(at + OBD, OBD), :]], axis=1).astype(BF16)
            sums = jnp.dot(hot, data, preferred_element_type=F32)
            for u in range(2):
                keep(k * 2 + u, sums[:, u * 128 : u * 128 + 128])
            return carry

        lax.fori_loop(0, 8, pair, 0)
        data = flat[pl.ds(16 * OBD, OBD), :].astype(BF16)
        keep(16, jnp.dot(hot, data, preferred_element_type=F32))

    def keep_other(r, sums):
        for q in range(8):
            core_s[q, r] = sums[q * 32 : q * 32 + 32].astype(BF16)

    def keep_own(r, sums):
        for q in range(8):
            own[q, r] = sums[q * 32 : q * 32 + 32]

    order = [1, 5, 2, 6, 3, 7, 0, 4]
    to_cells(for_other, keep_other)
    core_copies = {q: remote(core_s.at[q], core_r.at[q], core_ss.at[q], core_rs.at[q], at_core()) for q in order}
    for q in order:
        core_copies[q].start()
    to_cells(for_self, keep_own)

    copies1 = {}
    for q in order:
        half, step = q // 4, q % 4
        core_copies[q].wait_recv()
        if step:
            s1[q] = (own[q] + core_r[q].astype(F32)).astype(BF16)
            copies1[q] = remote(s1.at[q], r1.at[q], ss1.at[q], rs1.at[q], at_x(step) if half else at_y(step))
            copies1[q].start()
        else:
            acc1[half] = own[q] + core_r[q].astype(F32)

    copies2 = {}
    for half in range(2):
        for step in (1, 3, 2):
            copies1[half * 4 + step].wait_recv()
        acc = acc1[half]
        for step in range(1, 4):
            acc = acc + r1[half * 4 + step].astype(F32)
        acc2[pl.ds(half * PACKED, PACKED)] = acc[:, 0:8]
        for step in (2, 1, 3):
            q = half * 4 + step
            s2[q] = acc[:, step * 8 : step * 8 + 8].astype(BF16)
            copies2[q] = remote(s2.at[q], r2.at[q], ss2.at[q], rs2.at[q], at_y(step) if half else at_x(step))
            copies2[q].start()

    for half in range(2):
        for step in (1, 3, 2):
            copies2[half * 4 + step].wait_recv()
        span = pl.ds(half * PACKED, PACKED)
        acc = acc2[span]
        for step in range(1, 4):
            acc = acc + r2[half * 4 + step].astype(F32)
        acc2[span] = acc

    copies3 = {}
    wide = acc2.reshape(2 * PACKED * 8, 128)

    def cell(half, step):
        return wide[pl.ds(half * PACKED * 8 + step, PACKED, stride=8), :]

    for step in (4, 3, 5, 2, 6, 1, 7):
        for half in range(2):
            s3[step, half, 0:PACKED] = cell(half, step).astype(BF16)
        copies3[step] = remote(s3.at[step], r3.at[step], ss3.at[step], rs3.at[step], at_z(step))
        copies3[step].start()

    for copy in ens_copies:
        copy.wait_recv()
    ens_r[m] = ens_s[m]
    for g in range(2):
        raw = ens_r[:, g].astype(F32).reshape(MEMBERS, 1024)
        mean = jnp.sum(raw, axis=0, keepdims=True) / MEMBERS
        pert_s[g, 0:MEMBERS] = raw - mean
        pert_s[g, MEMBERS : MEMBERS + 8] = jnp.broadcast_to(mean, (8, 1024))

    for step in (1, 7, 2, 6, 3, 5, 4):
        copies3[step].wait_recv()
    both = []
    for half in range(2):
        total = cell(half, 0)
        for step in range(1, NZ):
            total = total + r3[step, half, 0:PACKED].astype(F32)
        both.append(transforms(total))

    means = []
    for g in range(2):
        result = jnp.dot(both[g], pert_s[g, 0:MEMBERS].astype(BF16), preferred_element_type=F32)
        for k in range(8):
            ana[k, g] = result[k * 8 : k * 8 + 8].astype(BF16)
        means.append(pert_s[g, MEMBERS : MEMBERS + 1] + result[64:65])
    out_copies = [
        remote(
            ana.at[lax.rem(m + s, 8)], out_ref.at[m], out_ss.at[s], out_rs.at[s], at_mem(s)
        )
        for s in (4, 3, 5, 2, 6, 1, 7)
    ]
    for copy in out_copies:
        copy.start()
    mine = pltpu.make_async_copy(ana.at[m], out_ref.at[m], self_sem)
    mine.start()
    mean_ref[...] = jnp.concatenate(means, axis=0).astype(BF16)

    for copy in ens_copies:
        copy.wait_send()
    for some in (core_copies, copies1, copies2, copies3):
        for copy in some.values():
            copy.wait_send()
    for copy in out_copies:
        copy.wait()
    mine.wait()


def body(ensemble, obs_members, obs_values, obs_weight, obs_count, obs_tile, obs_block, obs_turn):
    vmem, dma = pltpu.VMEM, pltpu.SemaphoreType.DMA
    whole = pl.BlockSpec(memory_space=pltpu.VMEM)
    arrived, mean = pl.pallas_call(
        kernel,
        name="letkf",
        out_shape=(
            jax.ShapeDtypeStruct((8, 2, 8, 1024), BF16),
            jax.ShapeDtypeStruct((2, 1024), BF16),
        ),
        in_specs=[whole, pl.BlockSpec(memory_space=pl.ANY)] + [whole] * 6,
        out_specs=(whole, whole),
        scratch_shapes=[
            vmem((OBD, MEMBERS, ROWS), BF16),
            vmem((8, 128, 128), F32),
            vmem((8, 2, 8, 1024), BF16),
            vmem((8, 2, 8, 1024), BF16),
            vmem((2, MEMBERS + 8, 1024), F32),
            vmem((OBD, ROWS), F32),
            vmem((PACKED * OBD, 128), F32),
            vmem((8, PACKED, 32, 128), BF16),
            vmem((8, PACKED, 32, 128), BF16),
            vmem((8, PACKED, 32, 128), F32),
            vmem((8, PACKED, 32, 128), BF16),
            vmem((8, PACKED, 32, 128), BF16),
            vmem((2, PACKED, 32, 128), F32),
            vmem((8, PACKED, 8, 128), BF16),
            vmem((8, PACKED, 8, 128), BF16),
            vmem((2 * PACKED, 8, 128), F32),
            vmem((NZ, 2, 24, 128), BF16),
            vmem((NZ, 2, 24, 128), BF16),
            vmem((8, 2, 8, 1024), BF16),
            dma((CHUNKS,)),
            dma((8,)), dma((8,)),
            dma((8,)), dma((8,)),
            dma((8,)), dma((8,)),
            dma((8,)), dma((8,)),
            dma((8,)), dma((8,)),
            dma((8,)), dma((8,)),
            dma(()),
        ],
        compiler_params=pltpu.CompilerParams(
            collective_id=0, has_side_effects=True, vmem_limit_bytes=48 << 20
        ),
    )(
        ensemble,
        obs_members,
        obs_values,
        obs_weight,
        obs_count.reshape(1, OBD),
        obs_tile.reshape(1, OBD),
        obs_block.reshape(1, OBD),
        obs_turn.reshape(1, OBD),
    )
    analysis = jnp.transpose(arrived.reshape(16, 8, 1024), (1, 0, 2))
    return analysis, mean


def solution(mesh):
    placed = (
        P("mem", "tile", None),
        P(("tile", "mem"), None, None),
        P(("tile", "mem"), None),
        P(("tile", "mem"), None),
        P(("tile", "mem")),
        P(("tile", "mem")),
        P(("tile", "mem")),
        P(("tile", "mem")),
    )
    return jax.shard_map(
        body,
        mesh=mesh,
        in_specs=placed,
        out_specs=(P("mem", "tile", None), P(("tile", "mem"), None)),
        check_vma=False,
    )
```

```python
import functools

import jax
import jax.numpy as jnp
from jax import lax
from jax.experimental import pallas as pl
from jax.experimental.pallas import tpu as pltpu
from jax.sharding import PartitionSpec as P

MESH = pl.DeviceIdType.MESH
MEMBERS = 64
ROWS = 128
OBD = 128
NS_STEPS = 6
NX, NY, NZ = 4, 4, 8
PACKED = 17
F32, BF16 = jnp.float32, jnp.bfloat16
CHUNKS = 8
EARLY = 4


def iota(shape, dim):
    return lax.broadcasted_iota(jnp.int32, shape, dim)


def nt(left, right):
    return lax.dot_general(left, right, (((1,), (1,)), ((), ())), preferred_element_type=F32)


def cell_rows(tile, block, turn, z, x, y, c):
    row, col = block // 4, block % 4
    new_row = jnp.where(turn == 0, row, jnp.where(turn == 1, col, jnp.where(turn == 2, 3 - row, 3 - col)))
    new_col = jnp.where(turn == 0, col, jnp.where(turn == 1, 3 - row, jnp.where(turn == 2, 3 - col, row)))
    dy = (new_row + NY - y) & 3
    dc = (new_col // 2 + c) & 1
    half = new_col & 1
    dz = ((tile // 4) + NZ - z) & 7
    dx = ((tile & 3) + NX - x) & 3
    inner = jnp.where(half == 0, dy * 32 + dx * 8, dx * 32 + dy * 8) + dz
    return dc * 256 + half * 128 + inner


def beside(left, right):
    return jnp.where(iota(left.shape, 1) < 64, left, pltpu.roll(right, 64, 1))


def stacked(value):
    left = iota(value.shape, 1) < 64
    zero = jnp.zeros_like(value)
    return jnp.concatenate([jnp.where(left, value, zero), jnp.where(left, zero, value)], axis=0)


def product(left, right):
    dot = functools.partial(jnp.dot, preferred_element_type=F32)
    high = left.astype(BF16)
    low = (left - high.astype(F32)).astype(BF16)
    wide = stacked(right)
    wide_high = wide.astype(BF16)
    wide_low = (wide - wide_high.astype(F32)).astype(BF16)
    first = dot(jnp.concatenate([high, low], axis=1), jnp.concatenate([wide_high, wide_high], axis=0))
    return first + dot(high, wide_low)


def half_matrix(main):
    lane, sub = iota((16, 128), 1), iota((16, 128), 0)
    col = lane & 15
    back = pltpu.roll(main, 112, 1)
    far = pltpu.roll(main, 64, 1)
    ba = pltpu.roll(main, 32, 1)
    aa = pltpu.roll(main, 16, 1)
    zero = jnp.zeros_like(main)
    row_d = jnp.where((lane < 48) | ((lane < 64) & (col < sub)), main, zero)
    row_c = jnp.where(lane < 32, far, jnp.where((lane < 48) & (col > sub), back, zero))
    row_b = jnp.where((lane < 16) | ((lane < 32) & (col < sub)), ba, zero)
    row_a = jnp.where((lane < 16) & (col > sub), aa, zero)
    return jnp.concatenate([row_a, row_b, row_c, row_d], axis=0)


def inverse_roots(first, second):
    one, two = half_matrix(first[:16]), half_matrix(second[:16])
    flipped = jnp.concatenate([one, two], axis=0).T[:64]
    lane, sub = iota((64, 128), 1), iota((64, 128), 0)
    eye = (lane & 63) == sub
    extra = [jnp.broadcast_to(v[16:17], (8, 128)) for v in (first, second)]
    diag = jnp.where(iota((8, 128), 1) < 64, pltpu.roll(extra[0], 64, 1), extra[1])[0:1]
    system = beside(one, two) + flipped + jnp.where(eye, diag + (MEMBERS - 1.0), 0.0)
    squares = jnp.sum(system * system, axis=0, keepdims=True)
    left = iota((1, 128), 1) < 64
    frob = jnp.sqrt(
        jnp.where(
            left,
            jnp.sum(jnp.where(left, squares, 0.0), axis=1, keepdims=True),
            jnp.sum(jnp.where(left, 0.0, squares), axis=1, keepdims=True),
        )
    )
    root = system / frob
    identity = jnp.where(eye, 1.0, 0.0)
    middle = 1.5 * identity - 0.5 * root
    inverse = middle
    root = product(root, middle)
    for sweep in range(1, NS_STEPS):
        middle = 1.5 * identity - 0.5 * product(inverse, root)
        if sweep < NS_STEPS - 1:
            root = product(root, middle)
        inverse = product(middle, inverse)
    return inverse / jnp.sqrt(frob), beside(extra[0], extra[1])


def kernel(
    ens_hbm, members_hbm, values_hbm, weight_hbm, count_hbm, tile_hbm, block_hbm, turn_hbm,
    out_hbm, mean_hbm,
    ens_ref, values_ref, weight_ref, count_ref, tile_ref, block_ref, turn_ref, mean_ref,
    obs, ens_f, ens_s, ens_r, means, pert_s, root_s, flat_f, flat_s, flat_r, rows_s, rows_r,
    s1, r1, acc1, s2, r2, acc2, s3, r3, ana,
    load_sem, small_sem, ens_ss, ens_rs, flat_ss, flat_rs, ss1, rs1, ss2, rs2, ss3, rs3, out_ss, out_rs, own_sem,
):
    t, m = lax.axis_index("tile"), lax.axis_index("mem")
    z, x, y, c = t // 4, t % 4, m // 2, m % 2

    def at_mem(step):
        return (t, lax.rem(m + step, 8))

    def at_core():
        return (t, y * 2 + 1 - c)

    def at_y(step):
        return (t, lax.rem(y + step, NY) * 2 + c)

    def at_x(step):
        return (z * 4 + lax.rem(x + step, NX), m)

    def at_z(step):
        return (lax.rem(z + step, NZ) * 4 + x, m)

    def remote(src, dst, send_sem, recv_sem, device):
        return pltpu.make_async_remote_copy(
            src_ref=src, dst_ref=dst, send_sem=send_sem, recv_sem=recv_sem, device_id=device, device_id_type=MESH
        )

    per = OBD // CHUNKS

    def load(i):
        span = pl.ds(i * per, per)
        return pltpu.make_async_copy(members_hbm.at[span], obs.at[span], load_sem.at[i])

    small = [
        pltpu.make_async_copy(source, target, small_sem.at[i])
        for i, (source, target) in enumerate(
            (
                (weight_hbm, weight_ref),
                (count_hbm, count_ref),
                (values_hbm, values_ref),
                (tile_hbm, tile_ref),
                (block_hbm, block_ref),
                (turn_hbm, turn_ref),
                (ens_hbm, ens_ref),
            )
        )
    ]
    for copy in small[:3]:
        copy.start()
    for i in range(CHUNKS):
        load(i).start()
    for copy in small[3:]:
        copy.start()

    barrier = pltpu.get_barrier_semaphore()
    partners = [at_mem(s) for s in range(1, 8)] + [at_x(s) for s in range(1, NX)] + [at_z(s) for s in range(1, NZ)]
    for device in partners:
        pl.semaphore_signal(barrier, inc=1, device_id=device, device_id_type=MESH)

    for copy in small[:3]:
        copy.wait()
    count = jnp.broadcast_to(count_ref[...].astype(F32), (OBD, OBD)).T
    usable = iota((OBD, ROWS), 1).astype(F32) < count
    root_s[...] = jnp.sqrt(jnp.where(usable, weight_ref[...], 0.0))

    lane, sub = iota((16, 128), 1), iota((16, 128), 0)
    col = lane & 15
    rolled_in = ((lane & 63) >= 48) & (col > sub)
    on_diag = (lane < 64) & (col == sub)

    def one_block(n, u):
        raw = obs[n].astype(F32)
        mean = jnp.sum(raw, axis=0, keepdims=True) / MEMBERS
        scale = root_s[pl.ds(n, 1), :]
        pert = ((raw - mean) * scale).astype(BF16)
        innov = ((values_ref[pl.ds(n, 1), :] - mean) * scale).astype(BF16)
        left = jnp.concatenate([pert, jnp.broadcast_to(innov, (16, ROWS))], axis=0)
        right = jnp.concatenate([pert, pert[:32], pert[:32]], axis=0)
        gram = nt(left, right)
        a, b, cc, d, p = gram[:16], gram[16:32], gram[32:48], gram[48:64], gram[64:65]
        rolled = pltpu.roll(jnp.where(lane < 64, cc, a), 16, 1)
        base = jnp.where(lane < 64, d, jnp.where(lane < 96, cc, b))
        flat_f[pl.ds(u, 16, stride=per), :] = jnp.where(rolled_in, rolled, base)
        four = jnp.where(lane < 16, a, jnp.where(lane < 32, b, jnp.where(lane < 48, cc, d)))
        diag = jnp.sum(jnp.where(on_diag, four, 0.0), axis=0, keepdims=True)
        flat_f[16 * per + u : 16 * per + u + 1, :] = jnp.where(lane[:1] < 64, p, pltpu.roll(diag, 64, 1))

    def chunk(i):
        load(i).wait()
        for u in range(per):
            one_block(i * per + u, u)
        flat_s[i] = flat_f[...].reshape(PACKED, per, 128).astype(BF16)

    def flat_copy(i):
        return remote(flat_s.at[i], flat_r.at[i], flat_ss.at[i], flat_rs.at[i], at_core())

    def plain(i, carry):
        chunk(i)
        return carry

    def with_copy(i, carry):
        chunk(i)
        flat_copy(i).start()
        return carry

    lax.fori_loop(0, EARLY, plain, 0)

    for copy in small[3:]:
        copy.wait()
    rows = cell_rows(tile_ref[...], block_ref[...], turn_ref[...], z, x, y, c).astype(F32)
    rows_s[...] = jnp.broadcast_to(rows - 256.0, (8, OBD))
    for j in range(8):
        for k in range(8):
            ens_f[j, pl.ds(k, 16, stride=8), :] = ens_ref[k, :, j * 128 : j * 128 + 128].astype(F32)
        ens_s[:, :, :, j * 128 : j * 128 + 128] = ens_f[j].reshape(8, 2, 8, 128).astype(BF16)

    pl.semaphore_wait(barrier, len(partners))
    rows_copy = remote(rows_s, rows_r, flat_ss.at[CHUNKS], flat_rs.at[CHUNKS], at_core())
    rows_copy.start()
    for i in range(EARLY):
        flat_copy(i).start()
    ens_copies = [
        remote(ens_s.at[lax.rem(m + s, 8)], ens_r.at[m], ens_ss.at[s], ens_rs.at[s], at_mem(s)) for s in range(1, 8)
    ]
    for copy in ens_copies:
        copy.start()
    lax.fori_loop(EARLY, CHUNKS, with_copy, 0)

    rows_copy.wait_recv()
    for i in range(CHUNKS):
        flat_copy(i).wait_recv()
    ids = iota((256, OBD), 0).astype(F32)
    hot = jnp.concatenate(
        [jnp.where(ids == rows, 1.0, 0.0).astype(BF16), jnp.where(ids == rows_r[0:1], 1.0, 0.0).astype(BF16)], axis=1
    )

    def keep(r, sums):
        for q in range(8):
            part = sums[q * 32 : q * 32 + 32]
            if q % 4:
                s1[q, r] = part.astype(BF16)
            else:
                acc1[q // 4, r] = part

    def both_cores(r):
        return jnp.concatenate([flat_s[:, r].reshape(OBD, 128), flat_r[:, r].reshape(OBD, 128)], axis=0)

    def pair(k, carry):
        data = jnp.concatenate([both_cores(k * 2), both_cores(k * 2 + 1)], axis=1)
        sums = jnp.dot(hot, data, preferred_element_type=F32)
        for u in range(2):
            keep(k * 2 + u, sums[:, u * 128 : u * 128 + 128])
        return carry

    groups = ((0, 8), (8, 9))

    def copy1(q, g):
        span = pl.ds(*groups[g])
        at, step = q * 2 + g, q % 4
        device = at_x(step) if q >= 4 else at_y(step)
        return remote(s1.at[q, span], r1.at[q, span], ss1.at[at], rs1.at[at], device)

    def copy2(q, g):
        span = pl.ds(*groups[g])
        at, step = q * 2 + g, q % 4
        device = at_y(step) if q >= 4 else at_x(step)
        return remote(s2.at[q, span], r2.at[q, span], ss2.at[at], rs2.at[at], device)

    def copy3(step, g):
        span = pl.ds(*((0, 8), (8, 16))[g])
        at = step * 2 + g
        return remote(s3.at[step, :, span], r3.at[step, :, span], ss3.at[at], rs3.at[at], at_z(step))

    order = (2, 6, 1, 5, 3, 7)
    for g in range(2):
        lax.fori_loop(g * 4, g * 4 + 4, pair, 0)
        if g:
            keep(16, jnp.dot(hot, both_cores(16), preferred_element_type=F32))
        for q in order:
            copy1(q, g).start()

    for g, (start, size) in enumerate(groups):
        span = pl.ds(start, size)
        for half in range(2):
            for step in (1, 3, 2):
                copy1(half * 4 + step, g).wait_recv()
            acc = acc1[half, span]
            for step in range(1, 4):
                acc = acc + r1[half * 4 + step, span].astype(F32)
            acc2[pl.ds(half * PACKED + start, size)] = acc[:, 0:8]
            for step in (2, 1, 3):
                q = half * 4 + step
                s2[q, span] = acc[:, step * 8 : step * 8 + 8].astype(BF16)
                copy2(q, g).start()

    wide = acc2.reshape(2 * PACKED * 8, 128)

    def cell(half, step, start, size):
        return wide[pl.ds((half * PACKED + start) * 8 + step, size, stride=8), :]

    for g, (start, size) in enumerate(groups):
        for half in range(2):
            for step in (1, 3, 2):
                copy2(half * 4 + step, g).wait_recv()
            span = pl.ds(half * PACKED + start, size)
            acc = acc2[span]
            for step in range(1, 4):
                acc = acc + r2[half * 4 + step, pl.ds(start, size)].astype(F32)
            acc2[span] = acc
        for step in (4, 3, 5, 2, 6, 1, 7):
            for half in range(2):
                s3[step, half, start : start + size] = cell(half, step, start, size).astype(BF16)
            copy3(step, g).start()

    for copy in ens_copies:
        copy.wait_recv()
    ens_r[m] = ens_s[m]
    for g in range(2):
        raw = ens_r[:, g].astype(F32).reshape(MEMBERS, 1024)
        mean = jnp.sum(raw, axis=0, keepdims=True) / MEMBERS
        means[g : g + 1] = mean
        pert_s[g * MEMBERS : g * MEMBERS + MEMBERS] = (raw - mean).astype(BF16)

    for g in range(2):
        for step in (1, 7, 2, 6, 3, 5, 4):
            copy3(step, g).wait_recv()
    total = []
    for half in range(2):
        value = cell(half, 0, 0, PACKED)
        for step in range(1, NZ):
            value = value + r3[step, half, 0:PACKED].astype(F32)
        total.append(value)
    roots, projection = inverse_roots(*total)

    spread = (jnp.sqrt(F32(MEMBERS - 1.0)) * roots).astype(BF16)
    result = jnp.dot(stacked(spread), pert_s[...], preferred_element_type=F32)
    for g in range(2):
        for k in range(8):
            at = g * MEMBERS + k * 8
            ana[k, g] = result[at : at + 8].astype(BF16)
    out_copies = [
        remote(ana.at[lax.rem(m + s, 8)], out_hbm.at[m], out_ss.at[s], out_rs.at[s], at_mem(s))
        for s in (4, 3, 5, 2, 6, 1, 7)
    ]
    for copy in out_copies:
        copy.start()
    mine = pltpu.make_async_copy(ana.at[m], out_hbm.at[m], own_sem.at[0])
    mine.start()

    weights = product(product(projection, roots), roots).astype(BF16)
    rise = jnp.dot(stacked(weights), pert_s[...], preferred_element_type=F32)
    mean_ref[...] = (means[0:2] + jnp.concatenate([rise[0:1], rise[8:9]], axis=0)).astype(BF16)
    mean_copy = pltpu.make_async_copy(mean_ref, mean_hbm, own_sem.at[1])
    mean_copy.start()

    for copy in out_copies:
        copy.wait()
    mine.wait()
    mean_copy.wait()
    for copy in ens_copies:
        copy.wait_send()
    rows_copy.wait_send()
    for i in range(CHUNKS):
        flat_copy(i).wait_send()
    for g in range(2):
        for q in order:
            copy1(q, g).wait_send()
            copy2(q, g).wait_send()
        for step in range(1, NZ):
            copy3(step, g).wait_send()


def body(ensemble, obs_members, obs_values, obs_weight, obs_count, obs_tile, obs_block, obs_turn):
    vmem, dma = pltpu.VMEM, pltpu.SemaphoreType.DMA
    whole = pl.BlockSpec(memory_space=pl.ANY)
    per = OBD // CHUNKS
    arrived, mean = pl.pallas_call(
        kernel,
        name="letkf",
        out_shape=(
            jax.ShapeDtypeStruct((8, 2, 8, 1024), BF16),
            jax.ShapeDtypeStruct((2, 1024), BF16),
        ),
        in_specs=[whole] * 8,
        out_specs=(whole, whole),
        scratch_shapes=[
            vmem((8, 16, 1024), BF16),
            vmem((OBD, ROWS), F32),
            vmem((OBD, ROWS), F32),
            vmem((1, OBD), jnp.int32),
            vmem((1, OBD), jnp.int32),
            vmem((1, OBD), jnp.int32),
            vmem((1, OBD), jnp.int32),
            vmem((2, 1024), BF16),
            vmem((OBD, MEMBERS, ROWS), BF16),
            vmem((8, 128, 128), F32),
            vmem((8, 2, 8, 1024), BF16),
            vmem((8, 2, 8, 1024), BF16),
            vmem((8, 1024), F32),
            vmem((2 * MEMBERS, 1024), BF16),
            vmem((OBD, ROWS), F32),
            vmem((PACKED * per, 128), F32),
            vmem((CHUNKS, PACKED, per, 128), BF16),
            vmem((CHUNKS, PACKED, per, 128), BF16),
            vmem((8, OBD), F32),
            vmem((8, OBD), F32),
            vmem((8, PACKED, 32, 128), BF16),
            vmem((8, PACKED, 32, 128), BF16),
            vmem((2, PACKED, 32, 128), F32),
            vmem((8, PACKED, 8, 128), BF16),
            vmem((8, PACKED, 8, 128), BF16),
            vmem((2 * PACKED, 8, 128), F32),
            vmem((NZ, 2, 24, 128), BF16),
            vmem((NZ, 2, 24, 128), BF16),
            vmem((8, 2, 8, 1024), BF16),
            dma((CHUNKS,)), dma((7,)),
            dma((8,)), dma((8,)),
            dma((CHUNKS + 1,)), dma((CHUNKS + 1,)),
            dma((16,)), dma((16,)),
            dma((16,)), dma((16,)),
            dma((16,)), dma((16,)),
            dma((8,)), dma((8,)),
            dma((2,)),
        ],
        compiler_params=pltpu.CompilerParams(
            collective_id=0, has_side_effects=True, vmem_limit_bytes=67043328
        ),
    )(
        ensemble,
        obs_members,
        obs_values,
        obs_weight,
        obs_count.reshape(1, OBD),
        obs_tile.reshape(1, OBD),
        obs_block.reshape(1, OBD),
        obs_turn.reshape(1, OBD),
    )
    analysis = jnp.transpose(arrived.reshape(16, 8, 1024), (1, 0, 2))
    return analysis, mean


def solution(mesh):
    placed = (
        P("mem", "tile", None),
        P(("tile", "mem"), None, None),
        P(("tile", "mem"), None),
        P(("tile", "mem"), None),
        P(("tile", "mem")),
        P(("tile", "mem")),
        P(("tile", "mem")),
        P(("tile", "mem")),
    )
    return jax.shard_map(
        body,
        mesh=mesh,
        in_specs=placed,
        out_specs=(P("mem", "tile", None), P(("tile", "mem"), None)),
        check_vma=False,
    )
```

```python
import functools

import jax
import jax.numpy as jnp
from jax import lax
from jax.experimental import pallas as pl
from jax.experimental.pallas import tpu as pltpu
from jax.sharding import PartitionSpec as P

MESH = pl.DeviceIdType.MESH
MEMBERS = 64
ROWS = 128
OBD = 128
NS_STEPS = 6
NX, NY, NZ = 4, 4, 8
PACKED = 17
F32, BF16 = jnp.float32, jnp.bfloat16
CHUNKS = 8
GROUPS = ((0, 6), (6, 6), (12, 5))
EARLY = 5


def iota(shape, dim):
    return lax.broadcasted_iota(jnp.int32, shape, dim)


def nt(left, right):
    return lax.dot_general(left, right, (((1,), (1,)), ((), ())), preferred_element_type=F32)


def cell_rows(tile, block, turn, z, x, y, c):
    row, col = block // 4, block % 4
    new_row = jnp.where(turn == 0, row, jnp.where(turn == 1, col, jnp.where(turn == 2, 3 - row, 3 - col)))
    new_col = jnp.where(turn == 0, col, jnp.where(turn == 1, 3 - row, jnp.where(turn == 2, 3 - col, row)))
    dy = (new_row + NY - y) & 3
    dc = (new_col // 2 + c) & 1
    half = new_col & 1
    dz = ((tile // 4) + NZ - z) & 7
    dx = ((tile & 3) + NX - x) & 3
    inner = jnp.where(half == 0, dy * 32 + dx * 8, dx * 32 + dy * 8) + dz
    return dc * 256 + half * 128 + inner


def beside(left, right):
    return jnp.where(iota(left.shape, 1) < 64, left, pltpu.roll(right, 64, 1))


def stacked(value):
    left = iota(value.shape, 1) < 64
    zero = jnp.zeros_like(value)
    return jnp.concatenate([jnp.where(left, value, zero), jnp.where(left, zero, value)], axis=0)


def product(left, right):
    dot = functools.partial(jnp.dot, preferred_element_type=F32)
    high = left.astype(BF16)
    low = (left - high.astype(F32)).astype(BF16)
    wide = stacked(right)
    wide_high = wide.astype(BF16)
    wide_low = (wide - wide_high.astype(F32)).astype(BF16)
    first = dot(jnp.concatenate([high, low], axis=1), jnp.concatenate([wide_high, wide_high], axis=0))
    return first + dot(high, wide_low)


def half_matrix(main):
    lane, sub = iota((16, 128), 1), iota((16, 128), 0)
    col = lane & 15
    back = pltpu.roll(main, 112, 1)
    far = pltpu.roll(main, 64, 1)
    ba = pltpu.roll(main, 32, 1)
    aa = pltpu.roll(main, 16, 1)
    zero = jnp.zeros_like(main)
    row_d = jnp.where((lane < 48) | ((lane < 64) & (col < sub)), main, zero)
    row_c = jnp.where(lane < 32, far, jnp.where((lane < 48) & (col > sub), back, zero))
    row_b = jnp.where((lane < 16) | ((lane < 32) & (col < sub)), ba, zero)
    row_a = jnp.where((lane < 16) & (col > sub), aa, zero)
    return jnp.concatenate([row_a, row_b, row_c, row_d], axis=0)


def inverse_roots(first, second):
    one, two = half_matrix(first[:16]), half_matrix(second[:16])
    flipped = jnp.concatenate([one, two], axis=0).T[:64]
    lane, sub = iota((64, 128), 1), iota((64, 128), 0)
    eye = (lane & 63) == sub
    extra = [jnp.broadcast_to(v[16:17], (8, 128)) for v in (first, second)]
    diag = jnp.where(iota((8, 128), 1) < 64, pltpu.roll(extra[0], 64, 1), extra[1])[0:1]
    system = beside(one, two) + flipped + jnp.where(eye, diag + (MEMBERS - 1.0), 0.0)
    squares = jnp.sum(system * system, axis=0, keepdims=True)
    left = iota((1, 128), 1) < 64
    frob = jnp.sqrt(
        jnp.where(
            left,
            jnp.sum(jnp.where(left, squares, 0.0), axis=1, keepdims=True),
            jnp.sum(jnp.where(left, 0.0, squares), axis=1, keepdims=True),
        )
    )
    root = system / frob
    identity = jnp.where(eye, 1.0, 0.0)
    middle = 1.5 * identity - 0.5 * root
    inverse = middle
    root = product(root, middle)
    for sweep in range(1, NS_STEPS):
        middle = 1.5 * identity - 0.5 * product(inverse, root)
        if sweep < NS_STEPS - 1:
            both = product(jnp.concatenate([root, inverse], axis=0), middle)
            root, inverse = both[:64], both[64:]
        else:
            inverse = product(inverse, middle)
    return inverse / jnp.sqrt(frob), beside(extra[0], extra[1])


def kernel(
    ens_hbm, members_hbm, values_hbm, weight_hbm, count_hbm, tile_hbm, block_hbm, turn_hbm,
    out_hbm, mean_hbm,
    ens_ref, values_ref, weight_ref, count_ref, tile_ref, block_ref, turn_ref, mean_ref,
    obs, ens_f, ens_s, ens_r, means, pert_s, root_s, flat_f, flat_s, flat_r, rows_s, rows_r,
    s1, r1, acc1, s2, r2, acc2, s3, r3, total, ana,
    load_sem, small_sem, ens_ss, ens_rs, flat_ss, flat_rs, ss1, rs1, ss2, rs2, ss3, rs3, out_ss, out_rs, own_sem,
):
    t, m = lax.axis_index("tile"), lax.axis_index("mem")
    z, x, y, c = t // 4, t % 4, m // 2, m % 2

    def at_mem(step):
        return (t, lax.rem(m + step, 8))

    def at_core():
        return (t, y * 2 + 1 - c)

    def at_y(step):
        return (t, lax.rem(y + step, NY) * 2 + c)

    def at_x(step):
        return (z * 4 + lax.rem(x + step, NX), m)

    def at_z(step):
        return (lax.rem(z + step, NZ) * 4 + x, m)

    def remote(src, dst, send_sem, recv_sem, device):
        return pltpu.make_async_remote_copy(
            src_ref=src, dst_ref=dst, send_sem=send_sem, recv_sem=recv_sem, device_id=device, device_id_type=MESH
        )

    per = OBD // CHUNKS

    def load(i):
        span = pl.ds(i * per, per)
        return pltpu.make_async_copy(members_hbm.at[span], obs.at[span], load_sem.at[i])

    small = [
        pltpu.make_async_copy(source, target, small_sem.at[i])
        for i, (source, target) in enumerate(
            (
                (weight_hbm, weight_ref),
                (count_hbm, count_ref),
                (values_hbm, values_ref),
                (tile_hbm, tile_ref),
                (block_hbm, block_ref),
                (turn_hbm, turn_ref),
                (ens_hbm, ens_ref),
            )
        )
    ]
    for copy in small[:3]:
        copy.start()
    for i in range(CHUNKS):
        load(i).start()
    for copy in small[3:]:
        copy.start()

    barrier = pltpu.get_barrier_semaphore()
    partners = [at_mem(s) for s in range(1, 8)] + [at_x(s) for s in range(1, NX)] + [at_z(s) for s in range(1, NZ)]
    for device in partners:
        pl.semaphore_signal(barrier, inc=1, device_id=device, device_id_type=MESH)

    for copy in small[:3]:
        copy.wait()
    count = jnp.broadcast_to(count_ref[...].astype(F32), (OBD, OBD)).T
    usable = iota((OBD, ROWS), 1).astype(F32) < count
    root_s[...] = jnp.sqrt(jnp.where(usable, weight_ref[...], 0.0))

    lane, sub = iota((16, 128), 1), iota((16, 128), 0)
    col = lane & 15
    rolled_in = ((lane & 63) >= 48) & (col > sub)
    on_diag = (lane < 64) & (col == sub)

    def one_block(n, u):
        raw = obs[n].astype(F32)
        mean = jnp.sum(raw, axis=0, keepdims=True) / MEMBERS
        scale = root_s[pl.ds(n, 1), :]
        pert = ((raw - mean) * scale).astype(BF16)
        innov = ((values_ref[pl.ds(n, 1), :] - mean) * scale).astype(BF16)
        left = jnp.concatenate([pert, jnp.broadcast_to(innov, (16, ROWS))], axis=0)
        gram = jnp.concatenate([nt(left, pert), jnp.zeros((80, 64), F32)], axis=1)
        a, b, cc, d, p = gram[:16], gram[16:32], gram[32:48], gram[48:64], gram[64:65]
        upper = rolled_in & (lane < 64)
        second = jnp.where(lane < 32, cc, jnp.where(upper, pltpu.roll(a, 48, 1), pltpu.roll(b, 32, 1)))
        first = jnp.where(upper, pltpu.roll(cc, 16, 1), d)
        flat_f[pl.ds(u, 16, stride=per), :] = jnp.where(lane < 64, first, pltpu.roll(second, 64, 1))
        four = jnp.where(lane < 16, a, jnp.where(lane < 32, b, jnp.where(lane < 48, cc, d)))
        diag = jnp.sum(jnp.where(on_diag, four, 0.0), axis=0, keepdims=True)
        flat_f[16 * per + u : 16 * per + u + 1, :] = jnp.where(lane[:1] < 64, p, pltpu.roll(diag, 64, 1))

    def chunk(i):
        load(i).wait()
        for u in range(per):
            one_block(i * per + u, u)
        flat_s[i] = flat_f[...].reshape(PACKED, per, 128).astype(BF16)

    def flat_copy(i):
        return remote(flat_s.at[i], flat_r.at[i], flat_ss.at[i], flat_rs.at[i], at_core())

    def plain(i, carry):
        chunk(i)
        return carry

    def with_copy(i, carry):
        chunk(i)
        flat_copy(i).start()
        return carry

    lax.fori_loop(0, EARLY, plain, 0)

    for copy in small[3:]:
        copy.wait()
    rows = cell_rows(tile_ref[...], block_ref[...], turn_ref[...], z, x, y, c).astype(F32)
    rows_s[...] = jnp.broadcast_to(rows - 256.0, (8, OBD))
    for j in range(8):
        for k in range(8):
            ens_f[j, pl.ds(k, 16, stride=8), :] = ens_ref[k, :, j * 128 : j * 128 + 128].astype(F32)
        ens_s[:, :, :, j * 128 : j * 128 + 128] = ens_f[j].reshape(8, 2, 8, 128).astype(BF16)

    pl.semaphore_wait(barrier, len(partners))
    rows_copy = remote(rows_s, rows_r, flat_ss.at[CHUNKS], flat_rs.at[CHUNKS], at_core())
    rows_copy.start()
    for i in range(EARLY):
        flat_copy(i).start()
    ens_copies = [
        remote(ens_s.at[lax.rem(m + s, 8)], ens_r.at[m], ens_ss.at[s], ens_rs.at[s], at_mem(s)) for s in range(1, 8)
    ]
    for copy in ens_copies:
        copy.start()
    lax.fori_loop(EARLY, CHUNKS, with_copy, 0)

    rows_copy.wait_recv()
    for i in range(CHUNKS):
        flat_copy(i).wait_recv()
    ids = iota((256, OBD), 0).astype(F32)
    hot = jnp.concatenate(
        [jnp.where(ids == rows, 1.0, 0.0).astype(BF16), jnp.where(ids == rows_r[0:1], 1.0, 0.0).astype(BF16)], axis=1
    )

    def keep(r, sums):
        for q in range(8):
            part = sums[q * 32 : q * 32 + 32]
            if q % 4:
                s1[q, r] = part.astype(BF16)
            else:
                acc1[q // 4, r] = part

    def both_cores(r):
        return jnp.concatenate([flat_s[:, r].reshape(OBD, 128), flat_r[:, r].reshape(OBD, 128)], axis=0)

    def pair(k, carry):
        data = jnp.concatenate([both_cores(k * 2), both_cores(k * 2 + 1)], axis=1)
        sums = jnp.dot(hot, data, preferred_element_type=F32)
        for u in range(2):
            keep(k * 2 + u, sums[:, u * 128 : u * 128 + 128])
        return carry

    def copy1(q, g):
        span = pl.ds(*GROUPS[g])
        at, step = q * len(GROUPS) + g, q % 4
        device = at_x(step) if q >= 4 else at_y(step)
        return remote(s1.at[q, span], r1.at[q, span], ss1.at[at], rs1.at[at], device)

    def copy2(q, g):
        span = pl.ds(*GROUPS[g])
        at, step = q * len(GROUPS) + g, q % 4
        device = at_y(step) if q >= 4 else at_x(step)
        return remote(s2.at[q, span], r2.at[q, span], ss2.at[at], rs2.at[at], device)

    def copy3(step, g):
        at = step * len(GROUPS) + g
        return remote(s3.at[step, g], r3.at[step, g], ss3.at[at], rs3.at[at], at_z(step))

    order = (2, 6, 1, 5, 3, 7)
    for g, (start, size) in enumerate(GROUPS):
        lax.fori_loop(start // 2, (start + size) // 2, pair, 0)
        if size % 2:
            keep(16, jnp.dot(hot, both_cores(16), preferred_element_type=F32))
        for q in order:
            copy1(q, g).start()

    for g, (start, size) in enumerate(GROUPS):
        span = pl.ds(start, size)
        for half in range(2):
            for step in (1, 3, 2):
                copy1(half * 4 + step, g).wait_recv()
            acc = acc1[half, span]
            for step in range(1, 4):
                acc = acc + r1[half * 4 + step, span].astype(F32)
            acc2[pl.ds(half * PACKED + start, size)] = acc[:, 0:8]
            for step in (2, 1, 3):
                q = half * 4 + step
                s2[q, span] = acc[:, step * 8 : step * 8 + 8].astype(BF16)
                copy2(q, g).start()

    wide = acc2.reshape(2 * PACKED * 8, 128)

    def cell(half, step, start, size):
        return wide[pl.ds((half * PACKED + start) * 8 + step, size, stride=8), :]

    for g, (start, size) in enumerate(GROUPS):
        for half in range(2):
            for step in (1, 3, 2):
                copy2(half * 4 + step, g).wait_recv()
            span = pl.ds(half * PACKED + start, size)
            acc = acc2[span]
            for step in range(1, 4):
                acc = acc + r2[half * 4 + step, pl.ds(start, size)].astype(F32)
            acc2[span] = acc
        for step in (4, 3, 5, 2, 6, 1, 7):
            for half in range(2):
                s3[step, g, half, 0:size] = cell(half, step, start, size).astype(BF16)
            copy3(step, g).start()

    for copy in ens_copies:
        copy.wait_recv()
    ens_r[m] = ens_s[m]
    for g in range(2):
        raw = ens_r[:, g].astype(F32).reshape(MEMBERS, 1024)
        mean = jnp.sum(raw, axis=0, keepdims=True) / MEMBERS
        means[g : g + 1] = mean
        pert_s[g * MEMBERS : g * MEMBERS + MEMBERS] = (raw - mean).astype(BF16)

    for g, (start, size) in enumerate(GROUPS):
        for step in (1, 7, 2, 6, 3, 5, 4):
            copy3(step, g).wait_recv()
        for half in range(2):
            value = cell(half, 0, start, size)
            for step in range(1, NZ):
                value = value + r3[step, g, half, 0:size].astype(F32)
            total[half, start : start + size] = value
    roots, projection = inverse_roots(total[0, 0:PACKED], total[1, 0:PACKED])

    spread = (jnp.sqrt(F32(MEMBERS - 1.0)) * roots).astype(BF16)
    result = jnp.dot(stacked(spread), pert_s[...], preferred_element_type=F32)
    for g in range(2):
        for k in range(8):
            at = g * MEMBERS + k * 8
            ana[k, g] = result[at : at + 8].astype(BF16)
    out_copies = [
        remote(ana.at[lax.rem(m + s, 8)], out_hbm.at[m], out_ss.at[s], out_rs.at[s], at_mem(s))
        for s in (4, 3, 5, 2, 6, 1, 7)
    ]
    for copy in out_copies:
        copy.start()
    mine = pltpu.make_async_copy(ana.at[m], out_hbm.at[m], own_sem.at[0])
    mine.start()

    weights = product(product(projection, roots), roots).astype(BF16)
    rise = jnp.dot(stacked(weights), pert_s[...], preferred_element_type=F32)
    mean_ref[...] = (means[0:2] + jnp.concatenate([rise[0:1], rise[8:9]], axis=0)).astype(BF16)
    mean_copy = pltpu.make_async_copy(mean_ref, mean_hbm, own_sem.at[1])
    mean_copy.start()

    for copy in out_copies:
        copy.wait()
    mine.wait()
    mean_copy.wait()
    for copy in ens_copies:
        copy.wait_send()
    rows_copy.wait_send()
    for i in range(CHUNKS):
        flat_copy(i).wait_send()
    for g in range(len(GROUPS)):
        for q in order:
            copy1(q, g).wait_send()
            copy2(q, g).wait_send()
        for step in range(1, NZ):
            copy3(step, g).wait_send()


def results(arrived_ref, mean_ref, out_hbm, mean_hbm, wide, turned, sem):
    copies = [pltpu.make_async_copy(mean_ref, mean_hbm, sem.at[8])]
    copies[0].start()
    for j in range(8):
        lanes = pl.ds(j * 128, 128)
        for g in range(16):
            wide[j, pl.ds(g, 8, stride=16), :] = arrived_ref[g, :, lanes].astype(F32)
        turned[:, :, lanes] = wide[j].reshape(8, 16, 128).astype(BF16)
        copies.append(pltpu.make_async_copy(turned.at[:, :, lanes], out_hbm.at[:, :, lanes], sem.at[j]))
        copies[-1].start()
    for copy in copies:
        copy.wait()


def body(ensemble, obs_members, obs_values, obs_weight, obs_count, obs_tile, obs_block, obs_turn):
    vmem, dma = pltpu.VMEM, pltpu.SemaphoreType.DMA
    whole = pl.BlockSpec(memory_space=pl.ANY)
    per = OBD // CHUNKS
    arrived, mean = pl.pallas_call(
        kernel,
        name="letkf",
        out_shape=(
            jax.ShapeDtypeStruct((8, 2, 8, 1024), BF16),
            jax.ShapeDtypeStruct((2, 1024), BF16),
        ),
        in_specs=[pl.BlockSpec(memory_space=pltpu.HBM)] * 8,
        out_specs=(whole, whole),
        scratch_shapes=[
            vmem((8, 16, 1024), BF16),
            vmem((OBD, ROWS), F32),
            vmem((OBD, ROWS), F32),
            vmem((1, OBD), jnp.int32),
            vmem((1, OBD), jnp.int32),
            vmem((1, OBD), jnp.int32),
            vmem((1, OBD), jnp.int32),
            vmem((2, 1024), BF16),
            vmem((OBD, MEMBERS, ROWS), BF16),
            vmem((8, 128, 128), F32),
            vmem((8, 2, 8, 1024), BF16),
            vmem((8, 2, 8, 1024), BF16),
            vmem((8, 1024), F32),
            vmem((2 * MEMBERS, 1024), BF16),
            vmem((OBD, ROWS), F32),
            vmem((PACKED * per, 128), F32),
            vmem((CHUNKS, PACKED, per, 128), BF16),
            vmem((CHUNKS, PACKED, per, 128), BF16),
            vmem((8, OBD), F32),
            vmem((8, OBD), F32),
            vmem((8, PACKED, 32, 128), BF16),
            vmem((8, PACKED, 32, 128), BF16),
            vmem((2, PACKED, 32, 128), F32),
            vmem((8, PACKED, 8, 128), BF16),
            vmem((8, PACKED, 8, 128), BF16),
            vmem((2 * PACKED, 8, 128), F32),
            vmem((NZ, len(GROUPS), 2, 8, 128), BF16),
            vmem((NZ, len(GROUPS), 2, 8, 128), BF16),
            vmem((2, 24, 128), F32),
            vmem((8, 2, 8, 1024), BF16),
            dma((CHUNKS,)), dma((7,)),
            dma((8,)), dma((8,)),
            dma((CHUNKS + 1,)), dma((CHUNKS + 1,)),
            dma((8 * len(GROUPS),)), dma((8 * len(GROUPS),)),
            dma((8 * len(GROUPS),)), dma((8 * len(GROUPS),)),
            dma((8 * len(GROUPS),)), dma((8 * len(GROUPS),)),
            dma((8,)), dma((8,)),
            dma((2,)),
        ],
        compiler_params=pltpu.CompilerParams(
            collective_id=0, has_side_effects=True, vmem_limit_bytes=48 << 20
        ),
    )(
        *(
            pltpu.with_memory_space_constraint(v, pltpu.HBM)
            for v in (
                ensemble,
                obs_members,
                obs_values,
                obs_weight,
                obs_count.reshape(1, OBD),
                obs_tile.reshape(1, OBD),
                obs_block.reshape(1, OBD),
                obs_turn.reshape(1, OBD),
            )
        )
    )
    return pl.pallas_call(
        results,
        name="results",
        out_shape=(
            jax.ShapeDtypeStruct((8, 16, 1024), BF16),
            jax.ShapeDtypeStruct((2, 1024), BF16),
        ),
        in_specs=[pl.BlockSpec(memory_space=pltpu.VMEM)] * 2,
        out_specs=(whole, whole),
        scratch_shapes=[vmem((8, 128, 128), F32), vmem((8, 16, 1024), BF16), dma((9,))],
        compiler_params=pltpu.CompilerParams(vmem_limit_bytes=16 << 20),
    )(arrived.reshape(16, 8, 1024), mean)


def solution(mesh):
    placed = (
        P("mem", "tile", None),
        P(("tile", "mem"), None, None),
        P(("tile", "mem"), None),
        P(("tile", "mem"), None),
        P(("tile", "mem")),
        P(("tile", "mem")),
        P(("tile", "mem")),
        P(("tile", "mem")),
    )
    return jax.shard_map(
        body,
        mesh=mesh,
        in_specs=placed,
        out_specs=(P("mem", "tile", None), P(("tile", "mem"), None)),
        check_vma=False,
    )
```

```python
import functools

import jax
import jax.numpy as jnp
from jax import lax
from jax.experimental import pallas as pl
from jax.experimental.pallas import tpu as pltpu
from jax.sharding import PartitionSpec as P

MESH = pl.DeviceIdType.MESH
MEMBERS = 64
ROWS = 128
OBD = 128
NS_STEPS = 6
NX, NY, NZ = 4, 4, 8
PACKED = 17
F32, BF16 = jnp.float32, jnp.bfloat16
CHUNKS = 8
UNITS = (15, 9, 10, 11, 12, 0, 1, 6, 13, 5, 8, 7, 14, 4, 3, 2)
GROUPS = ((0, 6), (6, 6), (12, 5))
EARLY = 5


def iota(shape, dim):
    return lax.broadcasted_iota(jnp.int32, shape, dim)


def nt(left, right):
    return lax.dot_general(left, right, (((1,), (1,)), ((), ())), preferred_element_type=F32)


def cell_rows(tile, block, turn, z, x, y, c):
    row, col = block // 4, block % 4
    new_row = jnp.where(turn == 0, row, jnp.where(turn == 1, col, jnp.where(turn == 2, 3 - row, 3 - col)))
    new_col = jnp.where(turn == 0, col, jnp.where(turn == 1, 3 - row, jnp.where(turn == 2, 3 - col, row)))
    dy = (new_row + NY - y) & 3
    dc = (new_col // 2 + c) & 1
    half = new_col & 1
    dz = ((tile // 4) + NZ - z) & 7
    dx = ((tile & 3) + NX - x) & 3
    place = dy * NX + dx
    unit = jnp.zeros_like(place)
    for k, value in enumerate(UNITS):
        unit = unit + jnp.where(place == k, value, 0)
    return dc * 256 + unit * 16 + half * 8 + dz


def beside(left, right):
    return jnp.where(iota(left.shape, 1) < 64, left, pltpu.roll(right, 64, 1))


def stacked(value):
    left = iota(value.shape, 1) < 64
    zero = jnp.zeros_like(value)
    return jnp.concatenate([jnp.where(left, value, zero), jnp.where(left, zero, value)], axis=0)


def product(left, right):
    dot = functools.partial(jnp.dot, preferred_element_type=F32)
    high = left.astype(BF16)
    low = (left - high.astype(F32)).astype(BF16)
    wide = stacked(right)
    wide_high = wide.astype(BF16)
    wide_low = (wide - wide_high.astype(F32)).astype(BF16)
    first = dot(jnp.concatenate([high, low], axis=1), jnp.concatenate([wide_high, wide_high], axis=0))
    return first + dot(high, wide_low)


def half_matrix(main):
    lane, sub = iota((16, 128), 1), iota((16, 128), 0)
    col = lane & 15
    back = pltpu.roll(main, 112, 1)
    far = pltpu.roll(main, 64, 1)
    ba = pltpu.roll(main, 32, 1)
    aa = pltpu.roll(main, 16, 1)
    zero = jnp.zeros_like(main)
    row_d = jnp.where((lane < 48) | ((lane < 64) & (col < sub)), main, zero)
    row_c = jnp.where(lane < 32, far, jnp.where((lane < 48) & (col > sub), back, zero))
    row_b = jnp.where((lane < 16) | ((lane < 32) & (col < sub)), ba, zero)
    row_a = jnp.where((lane < 16) & (col > sub), aa, zero)
    return jnp.concatenate([row_a, row_b, row_c, row_d], axis=0)


def inverse_roots(first, second):
    one, two = half_matrix(first[:16]), half_matrix(second[:16])
    flipped = jnp.concatenate([one, two], axis=0).T[:64]
    lane, sub = iota((64, 128), 1), iota((64, 128), 0)
    eye = (lane & 63) == sub
    extra = [jnp.broadcast_to(v[16:17], (8, 128)) for v in (first, second)]
    diag = jnp.where(iota((8, 128), 1) < 64, pltpu.roll(extra[0], 64, 1), extra[1])[0:1]
    system = beside(one, two) + flipped + jnp.where(eye, diag + (MEMBERS - 1.0), 0.0)
    squares = jnp.sum(system * system, axis=0, keepdims=True)
    left = iota((1, 128), 1) < 64
    frob = jnp.sqrt(
        jnp.where(
            left,
            jnp.sum(jnp.where(left, squares, 0.0), axis=1, keepdims=True),
            jnp.sum(jnp.where(left, 0.0, squares), axis=1, keepdims=True),
        )
    )
    root = system / frob
    identity = jnp.where(eye, 1.0, 0.0)
    middle = 1.5 * identity - 0.5 * root
    inverse = middle
    root = product(root, middle)
    for sweep in range(1, NS_STEPS):
        middle = 1.5 * identity - 0.5 * product(inverse, root)
        if sweep < NS_STEPS - 1:
            both = product(jnp.concatenate([root, inverse], axis=0), middle)
            root, inverse = both[:64], both[64:]
        else:
            inverse = product(inverse, middle)
    return inverse / jnp.sqrt(frob), beside(extra[0], extra[1])


def kernel(
    ens_hbm, members_hbm, values_hbm, weight_hbm, count_hbm, tile_hbm, block_hbm, turn_hbm,
    out_hbm, mean_hbm,
    ens_ref, values_ref, weight_ref, count_ref, tile_ref, block_ref, turn_ref, mean_ref,
    obs, ens_f, ens_s, ens_r, means, pert_s, root_s, flat_f, flat_s, flat_r, rows_s, rows_r,
    s1, r1, far1, near1, acc1, s2, r2, acc2, s3, r3, total, ana,
    load_sem, small_sem, ens_ss, ens_rs, flat_ss, flat_rs, ss1, rs1, ss2, rs2, ss3, rs3, out_ss, out_rs, own_sem,
):
    per = OBD // CHUNKS

    def load(i):
        span = pl.ds(i * per, per)
        return pltpu.make_async_copy(members_hbm.at[span], obs.at[span], load_sem.at[i])

    small = [
        pltpu.make_async_copy(source, target, small_sem.at[i])
        for i, (source, target) in enumerate(
            (
                (weight_hbm, weight_ref),
                (count_hbm, count_ref),
                (values_hbm, values_ref),
                (tile_hbm, tile_ref),
                (block_hbm, block_ref),
                (turn_hbm, turn_ref),
                (ens_hbm, ens_ref),
            )
        )
    ]
    for copy in small[:3]:
        copy.start()
    for i in range(CHUNKS):
        load(i).start()
    for copy in small[3:]:
        copy.start()

    t, m = lax.axis_index("tile"), lax.axis_index("mem")
    z, x, y, c = lax.div(t, 4), lax.rem(t, 4), lax.div(m, 2), lax.rem(m, 2)

    def at_mem(step):
        return (t, lax.rem(m + step, 8))

    def at_core():
        return (t, y * 2 + 1 - c)

    def at_y(step):
        return (t, lax.rem(y + step, NY) * 2 + c)

    def at_x(step):
        return (z * 4 + lax.rem(x + step, NX), m)

    def at_z(step):
        return (lax.rem(z + step, NZ) * 4 + x, m)

    def remote(src, dst, send_sem, recv_sem, device):
        return pltpu.make_async_remote_copy(
            src_ref=src, dst_ref=dst, send_sem=send_sem, recv_sem=recv_sem, device_id=device, device_id_type=MESH
        )

    barrier = pltpu.get_barrier_semaphore()
    partners = [at_mem(s) for s in range(1, 8)] + [at_x(s) for s in range(1, NX)] + [at_z(s) for s in range(1, NZ)]
    for device in partners:
        pl.semaphore_signal(barrier, inc=1, device_id=device, device_id_type=MESH)

    for copy in small[:3]:
        copy.wait()
    count = jnp.broadcast_to(count_ref[...].astype(F32), (OBD, OBD)).T
    usable = iota((OBD, ROWS), 1).astype(F32) < count
    root_s[...] = jnp.sqrt(jnp.where(usable, weight_ref[...], 0.0))

    lane, sub = iota((16, 128), 1), iota((16, 128), 0)
    col = lane & 15
    rolled_in = ((lane & 63) >= 48) & (col > sub)
    on_diag = (lane < 64) & (col == sub)

    def one_block(n, u):
        raw = obs[n].astype(F32)
        mean = jnp.sum(raw, axis=0, keepdims=True) / MEMBERS
        scale = root_s[pl.ds(n, 1), :]
        pert = ((raw - mean) * scale).astype(BF16)
        innov = ((values_ref[pl.ds(n, 1), :] - mean) * scale).astype(BF16)
        left = jnp.concatenate([pert, jnp.broadcast_to(innov, (16, ROWS))], axis=0)
        gram = jnp.concatenate([nt(left, pert), jnp.zeros((80, 64), F32)], axis=1)
        a, b, cc, d, p = gram[:16], gram[16:32], gram[32:48], gram[48:64], gram[64:65]
        upper = rolled_in & (lane < 64)
        second = jnp.where(lane < 32, cc, jnp.where(upper, pltpu.roll(a, 48, 1), pltpu.roll(b, 32, 1)))
        first = jnp.where(upper, pltpu.roll(cc, 16, 1), d)
        flat_f[pl.ds(u, 16, stride=per), :] = jnp.where(lane < 64, first, pltpu.roll(second, 64, 1))
        four = jnp.where(lane < 16, a, jnp.where(lane < 32, b, jnp.where(lane < 48, cc, d)))
        diag = jnp.sum(jnp.where(on_diag, four, 0.0), axis=0, keepdims=True)
        flat_f[16 * per + u : 16 * per + u + 1, :] = jnp.where(lane[:1] < 64, p, pltpu.roll(diag, 64, 1))

    def chunk(i):
        load(i).wait()
        for u in range(per):
            one_block(i * per + u, u)
        flat_s[i] = flat_f[...].reshape(PACKED, per, 128).astype(BF16)

    def flat_copy(i):
        return remote(flat_s.at[i], flat_r.at[i], flat_ss.at[i], flat_rs.at[i], at_core())

    def plain(i, carry):
        chunk(i)
        return carry

    def with_copy(i, carry):
        chunk(i)
        flat_copy(i).start()
        return carry

    lax.fori_loop(0, EARLY, plain, 0)

    for copy in small[3:6]:
        copy.wait()
    rows = cell_rows(tile_ref[...], block_ref[...], turn_ref[...], z, x, y, c).astype(F32)
    rows_s[...] = jnp.broadcast_to(rows - 256.0, (8, OBD))

    small[6].wait()
    for j in range(8):
        for k in range(8):
            ens_f[j, pl.ds(k, 16, stride=8), :] = ens_ref[k, :, j * 128 : j * 128 + 128].astype(F32)
        ens_s[:, :, :, j * 128 : j * 128 + 128] = ens_f[j].reshape(8, 2, 8, 128).astype(BF16)
    pl.semaphore_wait(barrier, len(partners))
    rows_copy = remote(rows_s, rows_r, flat_ss.at[CHUNKS], flat_rs.at[CHUNKS], at_core())
    rows_copy.start()
    for i in range(EARLY):
        flat_copy(i).start()
    ens_copies = [
        remote(ens_s.at[lax.rem(m + s, 8)], ens_r.at[m], ens_ss.at[s], ens_rs.at[s], at_mem(s)) for s in range(1, 8)
    ]
    for copy in ens_copies:
        copy.start()
    lax.fori_loop(EARLY, CHUNKS, with_copy, 0)

    rows_copy.wait_recv()
    for i in range(CHUNKS):
        flat_copy(i).wait_recv()
    ids = iota((256, OBD), 0).astype(F32)
    hot = jnp.concatenate(
        [jnp.where(ids == rows, 1.0, 0.0).astype(BF16), jnp.where(ids == rows_r[0:1], 1.0, 0.0).astype(BF16)], axis=1
    )

    def keep(r, sums):
        for q in range(4):
            s1[q, r] = sums[q * 32 : q * 32 + 32].astype(BF16)
        far1[0, r] = sums[128:136].astype(BF16)
        far1[1, r] = sums[136:144].astype(BF16)
        for k in range(7):
            acc1[k, r] = sums[144 + k * 16 : 160 + k * 16]

    def both_cores(r):
        return jnp.concatenate([flat_s[:, r].reshape(OBD, 128), flat_r[:, r].reshape(OBD, 128)], axis=0)

    def pair(k, carry):
        data = jnp.concatenate([both_cores(k * 2), both_cores(k * 2 + 1)], axis=1)
        sums = jnp.dot(hot, data, preferred_element_type=F32)
        for u in range(2):
            keep(k * 2 + u, sums[:, u * 128 : u * 128 + 128])
        return carry

    def copy1(q, g):
        span = pl.ds(*GROUPS[g])
        at = q * len(GROUPS) + g
        device = (at_y(1), at_y(3), at_x(1), at_x(3), at_y(2), at_x(2))[q]
        source, target = (s1.at[q, span], r1.at[q, span]) if q < 4 else (far1.at[q - 4, span], near1.at[q - 4, span])
        return remote(source, target, ss1.at[at], rs1.at[at], device)

    def copy2(q, g):
        span = pl.ds(*GROUPS[g])
        at = q * len(GROUPS) + g
        return remote(s2.at[q, span], r2.at[q, span], ss2.at[at], rs2.at[at], at_x(q + 1) if q < 3 else at_y(q - 2))

    def copy3(step, g):
        at = step * len(GROUPS) + g
        return remote(s3.at[step, g], r3.at[step, g], ss3.at[at], rs3.at[at], at_z(step))

    order = (4, 5, 0, 1, 2, 3)
    for g, (start, size) in enumerate(GROUPS):
        lax.fori_loop(start // 2, (start + size) // 2, pair, 0)
        if size % 2:
            keep(16, jnp.dot(hot, both_cores(16), preferred_element_type=F32))
        for q in order:
            copy1(q, g).start()

    for g, (start, size) in enumerate(GROUPS):
        span = pl.ds(start, size)
        for q in range(4):
            copy1(q, g).wait_recv()

        def come(q, unit, span=span):
            return r1[q, span, unit * 16 : unit * 16 + 16].astype(F32)

        for q, source, unit in ((0, 0, 0), (2, 1, 0), (3, 3, 0), (5, 2, 0)):
            s2[q, span] = (acc1[q, span] + come(source, unit)).astype(BF16)
            copy2(q, g).start()
        for q in (4, 5):
            copy1(q, g).wait_recv()
        for axis, (q, one, two) in enumerate(((1, 0, 1), (4, 2, 3))):
            value = acc1[q, span] + come(one, 1) + come(two, 1)
            far = near1[axis, span].astype(F32)
            parts = [value[:, 0:8], value[:, 8:16]]
            parts[axis] = parts[axis] + far
            s2[q, span, 0:8] = parts[0].astype(BF16)
            s2[q, span, 8:16] = parts[1].astype(BF16)
            copy2(q, g).start()

    wide = acc2.reshape(2 * PACKED * 8, 128)

    def cell(half, step, start, size):
        return wide[pl.ds((half * PACKED + start) * 8 + step, size, stride=8), :]

    for g, (start, size) in enumerate(GROUPS):
        value = acc1[6, pl.ds(start, size)]
        for q in (0, 2, 3, 5, 1, 4):
            copy2(q, g).wait_recv()
            value = value + r2[q, pl.ds(start, size)].astype(F32)
        for half in range(2):
            acc2[pl.ds(half * PACKED + start, size)] = value[:, half * 8 : half * 8 + 8]
        for step in (4, 3, 5, 2, 6, 1, 7):
            for half in range(2):
                s3[step, g, half, 0:size] = cell(half, step, start, size).astype(BF16)
            copy3(step, g).start()

    for copy in ens_copies:
        copy.wait_recv()
    ens_r[m] = ens_s[m]
    for g in range(2):
        raw = ens_r[:, g].astype(F32).reshape(MEMBERS, 1024)
        mean = jnp.sum(raw, axis=0, keepdims=True) / MEMBERS
        means[g : g + 1] = mean
        pert_s[g * MEMBERS : g * MEMBERS + MEMBERS] = (raw - mean).astype(BF16)

    for g, (start, size) in enumerate(GROUPS):
        for step in (1, 7, 2, 6, 3, 5, 4):
            copy3(step, g).wait_recv()
        for half in range(2):
            value = cell(half, 0, start, size)
            for step in range(1, NZ):
                value = value + r3[step, g, half, 0:size].astype(F32)
            total[half, start : start + size] = value
    roots, projection = inverse_roots(total[0, 0:PACKED], total[1, 0:PACKED])

    spread = (jnp.sqrt(F32(MEMBERS - 1.0)) * roots).astype(BF16)
    result = jnp.dot(stacked(spread), pert_s[...], preferred_element_type=F32)
    for g in range(2):
        for k in range(8):
            at = g * MEMBERS + k * 8
            ana[k, g] = result[at : at + 8].astype(BF16)
    out_copies = [
        remote(ana.at[lax.rem(m + s, 8)], out_hbm.at[m], out_ss.at[s], out_rs.at[s], at_mem(s))
        for s in (4, 3, 5, 2, 6, 1, 7)
    ]
    for copy in out_copies:
        copy.start()
    mine = pltpu.make_async_copy(ana.at[m], out_hbm.at[m], own_sem.at[0])
    mine.start()

    weights = product(product(projection, roots), roots).astype(BF16)
    rise = jnp.dot(stacked(weights), pert_s[...], preferred_element_type=F32)
    mean_ref[...] = (means[0:2] + jnp.concatenate([rise[0:1], rise[8:9]], axis=0)).astype(BF16)
    mean_copy = pltpu.make_async_copy(mean_ref, mean_hbm, own_sem.at[1])
    mean_copy.start()

    for copy in ens_copies:
        copy.wait_send()
    rows_copy.wait_send()
    for i in range(CHUNKS):
        flat_copy(i).wait_send()
    for g in range(len(GROUPS)):
        for q in order:
            copy1(q, g).wait_send()
            copy2(q, g).wait_send()
        for step in range(1, NZ):
            copy3(step, g).wait_send()
    for copy in out_copies:
        copy.wait()
    mine.wait()
    mean_copy.wait()


def results(arrived_ref, mean_ref, out_hbm, mean_hbm, wide, turned, sem):
    copies = [pltpu.make_async_copy(mean_ref, mean_hbm, sem.at[8])]
    copies[0].start()
    for j in range(8):
        lanes = pl.ds(j * 128, 128)
        for g in range(16):
            wide[j, pl.ds(g, 8, stride=16), :] = arrived_ref[g, :, lanes].astype(F32)
        turned[:, :, lanes] = wide[j].reshape(8, 16, 128).astype(BF16)
        copies.append(pltpu.make_async_copy(turned.at[:, :, lanes], out_hbm.at[:, :, lanes], sem.at[j]))
        copies[-1].start()
    for copy in copies:
        copy.wait()


def body(ensemble, obs_members, obs_values, obs_weight, obs_count, obs_tile, obs_block, obs_turn):
    vmem, dma = pltpu.VMEM, pltpu.SemaphoreType.DMA
    whole = pl.BlockSpec(memory_space=pl.ANY)
    per = OBD // CHUNKS
    arrived, mean = pl.pallas_call(
        kernel,
        name="letkf",
        out_shape=(
            jax.ShapeDtypeStruct((8, 2, 8, 1024), BF16),
            jax.ShapeDtypeStruct((2, 1024), BF16),
        ),
        in_specs=[pl.BlockSpec(memory_space=pltpu.HBM)] * 8,
        out_specs=(whole, whole),
        scratch_shapes=[
            vmem((8, 16, 1024), BF16),
            vmem((OBD, ROWS), F32),
            vmem((OBD, ROWS), F32),
            vmem((1, OBD), jnp.int32),
            vmem((1, OBD), jnp.int32),
            vmem((1, OBD), jnp.int32),
            vmem((1, OBD), jnp.int32),
            vmem((2, 1024), BF16),
            vmem((OBD, MEMBERS, ROWS), BF16),
            vmem((8, 128, 128), F32),
            vmem((8, 2, 8, 1024), BF16),
            vmem((8, 2, 8, 1024), BF16),
            vmem((8, 1024), F32),
            vmem((2 * MEMBERS, 1024), BF16),
            vmem((OBD, ROWS), F32),
            vmem((PACKED * per, 128), F32),
            vmem((CHUNKS, PACKED, per, 128), BF16),
            vmem((CHUNKS, PACKED, per, 128), BF16),
            vmem((8, OBD), F32),
            vmem((8, OBD), F32),
            vmem((4, PACKED, 32, 128), BF16),
            vmem((4, PACKED, 32, 128), BF16),
            vmem((2, PACKED, 8, 128), BF16),
            vmem((2, PACKED, 8, 128), BF16),
            vmem((7, PACKED, 16, 128), F32),
            vmem((6, PACKED, 16, 128), BF16),
            vmem((6, PACKED, 16, 128), BF16),
            vmem((2 * PACKED, 8, 128), F32),
            vmem((NZ, len(GROUPS), 2, 8, 128), BF16),
            vmem((NZ, len(GROUPS), 2, 8, 128), BF16),
            vmem((2, 24, 128), F32),
            vmem((8, 2, 8, 1024), BF16),
            dma((CHUNKS,)), dma((7,)),
            dma((8,)), dma((8,)),
            dma((CHUNKS + 1,)), dma((CHUNKS + 1,)),
            dma((8 * len(GROUPS),)), dma((8 * len(GROUPS),)),
            dma((8 * len(GROUPS),)), dma((8 * len(GROUPS),)),
            dma((8 * len(GROUPS),)), dma((8 * len(GROUPS),)),
            dma((8,)), dma((8,)),
            dma((2,)),
        ],
        compiler_params=pltpu.CompilerParams(
            collective_id=0, has_side_effects=True, vmem_limit_bytes=48 << 20
        ),
    )(
        *(
            pltpu.with_memory_space_constraint(v, pltpu.HBM)
            for v in (
                ensemble,
                obs_members,
                obs_values,
                obs_weight,
                obs_count.reshape(1, OBD),
                obs_tile.reshape(1, OBD),
                obs_block.reshape(1, OBD),
                obs_turn.reshape(1, OBD),
            )
        )
    )
    return pl.pallas_call(
        results,
        name="results",
        out_shape=(
            jax.ShapeDtypeStruct((8, 16, 1024), BF16),
            jax.ShapeDtypeStruct((2, 1024), BF16),
        ),
        in_specs=[pl.BlockSpec(memory_space=pltpu.VMEM)] * 2,
        out_specs=(whole, whole),
        scratch_shapes=[vmem((8, 128, 128), F32), vmem((8, 16, 1024), BF16), dma((9,))],
        compiler_params=pltpu.CompilerParams(vmem_limit_bytes=16 << 20),
    )(arrived.reshape(16, 8, 1024), mean)


def solution(mesh):
    placed = (
        P("mem", "tile", None),
        P(("tile", "mem"), None, None),
        P(("tile", "mem"), None),
        P(("tile", "mem"), None),
        P(("tile", "mem")),
        P(("tile", "mem")),
        P(("tile", "mem")),
        P(("tile", "mem")),
    )
    return jax.shard_map(
        body,
        mesh=mesh,
        in_specs=placed,
        out_specs=(P("mem", "tile", None), P(("tile", "mem"), None)),
        check_vma=False,
    )
```

```python
import functools

import jax
import jax.numpy as jnp
from jax import lax
from jax.experimental import pallas as pl
from jax.experimental.pallas import tpu as pltpu
from jax.sharding import PartitionSpec as P

MESH = pl.DeviceIdType.MESH
MEMBERS = 64
ROWS = 128
OBD = 128
NS_STEPS = 6
NX, NY, NZ = 4, 4, 8
PACKED = 17
F32, BF16 = jnp.float32, jnp.bfloat16
CHUNKS = 8
UNITS = (15, 9, 10, 11, 12, 0, 1, 6, 13, 5, 8, 7, 14, 4, 3, 2)
GROUPS = ((0, 4), (4, 6), (10, 7))
EARLY = 5


def iota(shape, dim):
    return lax.broadcasted_iota(jnp.int32, shape, dim)


def nt(left, right):
    return lax.dot_general(left, right, (((1,), (1,)), ((), ())), preferred_element_type=F32)


def cell_rows(tile, block, turn, z, x, y, c):
    row, col = block // 4, block % 4
    new_row = jnp.where(turn == 0, row, jnp.where(turn == 1, col, jnp.where(turn == 2, 3 - row, 3 - col)))
    new_col = jnp.where(turn == 0, col, jnp.where(turn == 1, 3 - row, jnp.where(turn == 2, 3 - col, row)))
    dy = (new_row + NY - y) & 3
    dc = (new_col // 2 + c) & 1
    half = new_col & 1
    dz = ((tile // 4) + NZ - z) & 7
    dx = ((tile & 3) + NX - x) & 3
    place = dy * NX + dx
    unit = jnp.zeros_like(place)
    for k, value in enumerate(UNITS):
        unit = unit + jnp.where(place == k, value, 0)
    return dc * 256 + unit * 16 + half * 8 + dz


def beside(left, right):
    return jnp.where(iota(left.shape, 1) < 64, left, pltpu.roll(right, 64, 1))


def stacked(value):
    left = iota(value.shape, 1) < 64
    zero = jnp.zeros_like(value)
    return jnp.concatenate([jnp.where(left, value, zero), jnp.where(left, zero, value)], axis=0)


def product(left, right):
    dot = functools.partial(jnp.dot, preferred_element_type=F32)
    high = left.astype(BF16)
    low = (left - high.astype(F32)).astype(BF16)
    wide = stacked(right)
    wide_high = wide.astype(BF16)
    wide_low = (wide - wide_high.astype(F32)).astype(BF16)
    first = dot(jnp.concatenate([high, low], axis=1), jnp.concatenate([wide_high, wide_high], axis=0))
    return first + dot(high, wide_low)


def half_matrix(main):
    lane, sub = iota((16, 128), 1), iota((16, 128), 0)
    col = lane & 15
    back = pltpu.roll(main, 112, 1)
    far = pltpu.roll(main, 64, 1)
    ba = pltpu.roll(main, 32, 1)
    aa = pltpu.roll(main, 16, 1)
    zero = jnp.zeros_like(main)
    row_d = jnp.where((lane < 48) | ((lane < 64) & (col < sub)), main, zero)
    row_c = jnp.where(lane < 32, far, jnp.where((lane < 48) & (col > sub), back, zero))
    row_b = jnp.where((lane < 16) | ((lane < 32) & (col < sub)), ba, zero)
    row_a = jnp.where((lane < 16) & (col > sub), aa, zero)
    return jnp.concatenate([row_a, row_b, row_c, row_d], axis=0)


def inverse_roots(first, second):
    one, two = half_matrix(first[:16]), half_matrix(second[:16])
    flipped = jnp.concatenate([one, two], axis=0).T[:64]
    lane, sub = iota((64, 128), 1), iota((64, 128), 0)
    eye = (lane & 63) == sub
    extra = [jnp.broadcast_to(v[16:17], (8, 128)) for v in (first, second)]
    diag = jnp.where(iota((8, 128), 1) < 64, pltpu.roll(extra[0], 64, 1), extra[1])[0:1]
    system = beside(one, two) + flipped + jnp.where(eye, diag + (MEMBERS - 1.0), 0.0)
    squares = jnp.sum(system * system, axis=0, keepdims=True)
    left = iota((1, 128), 1) < 64
    frob = jnp.sqrt(
        jnp.where(
            left,
            jnp.sum(jnp.where(left, squares, 0.0), axis=1, keepdims=True),
            jnp.sum(jnp.where(left, 0.0, squares), axis=1, keepdims=True),
        )
    )
    root = system / frob
    identity = jnp.where(eye, 1.0, 0.0)
    middle = 1.5 * identity - 0.5 * root
    inverse = middle
    root = product(root, middle)
    for sweep in range(1, NS_STEPS):
        middle = 1.5 * identity - 0.5 * product(inverse, root)
        if sweep < NS_STEPS - 1:
            both = product(jnp.concatenate([root, inverse], axis=0), middle)
            root, inverse = both[:64], both[64:]
        else:
            inverse = product(inverse, middle)
    return inverse / jnp.sqrt(frob), beside(extra[0], extra[1])


def kernel(
    ens_hbm, members_hbm, values_hbm, weight_hbm, count_hbm, tile_hbm, block_hbm, turn_hbm,
    out_hbm, mean_hbm,
    ens_ref, values_ref, weight_ref, count_ref, tile_ref, block_ref, turn_ref, mean_ref,
    obs, ens_f, ens_s, ens_r, means, pert_s, root_s, flat_f, flat_s, flat_r, rows_s, rows_r,
    s1, r1, far1, near1, acc1, s2, r2, acc2, s3, r3, total, ana,
    load_sem, small_sem, ens_ss, ens_rs, flat_ss, flat_rs, ss1, rs1, ss2, rs2, ss3, rs3, out_ss, out_rs, own_sem,
):
    per = OBD // CHUNKS

    def load(i):
        span = pl.ds(i * per, per)
        return pltpu.make_async_copy(members_hbm.at[span], obs.at[span], load_sem.at[i])

    small = [
        pltpu.make_async_copy(source, target, small_sem.at[i])
        for i, (source, target) in enumerate(
            (
                (weight_hbm, weight_ref),
                (count_hbm, count_ref),
                (values_hbm, values_ref),
                (tile_hbm, tile_ref),
                (block_hbm, block_ref),
                (turn_hbm, turn_ref),
                (ens_hbm, ens_ref),
            )
        )
    ]
    for copy in small[:3]:
        copy.start()
    for i in range(CHUNKS):
        load(i).start()
    for copy in small[3:]:
        copy.start()

    t, m = lax.axis_index("tile"), lax.axis_index("mem")
    z, x, y, c = lax.div(t, 4), lax.rem(t, 4), lax.div(m, 2), lax.rem(m, 2)

    def at_mem(step):
        return (t, lax.rem(m + step, 8))

    def at_core():
        return (t, y * 2 + 1 - c)

    def at_y(step):
        return (t, lax.rem(y + step, NY) * 2 + c)

    def at_x(step):
        return (z * 4 + lax.rem(x + step, NX), m)

    def at_z(step):
        return (lax.rem(z + step, NZ) * 4 + x, m)

    def remote(src, dst, send_sem, recv_sem, device):
        return pltpu.make_async_remote_copy(
            src_ref=src, dst_ref=dst, send_sem=send_sem, recv_sem=recv_sem, device_id=device, device_id_type=MESH
        )

    barrier = pltpu.get_barrier_semaphore()
    partners = [at_mem(s) for s in range(1, 8)] + [at_x(s) for s in range(1, NX)] + [at_z(s) for s in range(1, NZ)]
    for device in partners:
        pl.semaphore_signal(barrier, inc=1, device_id=device, device_id_type=MESH)

    for copy in small[:3]:
        copy.wait()
    count = jnp.broadcast_to(count_ref[...].astype(F32), (OBD, OBD)).T
    usable = iota((OBD, ROWS), 1).astype(F32) < count
    root_s[...] = jnp.sqrt(jnp.where(usable, weight_ref[...], 0.0))

    lane, sub = iota((16, 128), 1), iota((16, 128), 0)
    col = lane & 15
    rolled_in = ((lane & 63) >= 48) & (col > sub)
    on_diag = (lane < 64) & (col == sub)

    def one_block(n, u):
        raw = obs[n].astype(F32)
        mean = jnp.sum(raw, axis=0, keepdims=True) / MEMBERS
        scale = root_s[pl.ds(n, 1), :]
        pert = ((raw - mean) * scale).astype(BF16)
        innov = ((values_ref[pl.ds(n, 1), :] - mean) * scale).astype(BF16)
        left = jnp.concatenate([pert, jnp.broadcast_to(innov, (16, ROWS))], axis=0)
        gram = jnp.concatenate([nt(left, pert), jnp.zeros((80, 64), F32)], axis=1)
        a, b, cc, d, p = gram[:16], gram[16:32], gram[32:48], gram[48:64], gram[64:65]
        upper = rolled_in & (lane < 64)
        second = jnp.where(lane < 32, cc, jnp.where(upper, pltpu.roll(a, 48, 1), pltpu.roll(b, 32, 1)))
        first = jnp.where(upper, pltpu.roll(cc, 16, 1), d)
        flat_f[pl.ds(u, 16, stride=per), :] = jnp.where(lane < 64, first, pltpu.roll(second, 64, 1))
        four = jnp.where(lane < 16, a, jnp.where(lane < 32, b, jnp.where(lane < 48, cc, d)))
        diag = jnp.sum(jnp.where(on_diag, four, 0.0), axis=0, keepdims=True)
        flat_f[16 * per + u : 16 * per + u + 1, :] = jnp.where(lane[:1] < 64, p, pltpu.roll(diag, 64, 1))

    def chunk(i):
        load(i).wait()
        for u in range(per):
            one_block(i * per + u, u)
        flat_s[i] = flat_f[...].reshape(PACKED, per, 128).astype(BF16)

    def flat_copy(i):
        return remote(flat_s.at[i], flat_r.at[i], flat_ss.at[i], flat_rs.at[i], at_core())

    def plain(i, carry):
        chunk(i)
        return carry

    def with_copy(i, carry):
        chunk(i)
        flat_copy(i).start()
        return carry

    lax.fori_loop(0, EARLY, plain, 0)

    for copy in small[3:6]:
        copy.wait()
    rows = cell_rows(tile_ref[...], block_ref[...], turn_ref[...], z, x, y, c).astype(F32)
    rows_s[...] = jnp.broadcast_to(rows - 256.0, (8, OBD))

    small[6].wait()
    for j in range(8):
        for k in range(8):
            ens_f[j, pl.ds(k, 16, stride=8), :] = ens_ref[k, :, j * 128 : j * 128 + 128].astype(F32)
        ens_s[:, :, :, j * 128 : j * 128 + 128] = ens_f[j].reshape(8, 2, 8, 128).astype(BF16)
    pl.semaphore_wait(barrier, len(partners))
    rows_copy = remote(rows_s, rows_r, flat_ss.at[CHUNKS], flat_rs.at[CHUNKS], at_core())
    rows_copy.start()
    for i in range(EARLY):
        flat_copy(i).start()
    ens_copies = [
        remote(ens_s.at[lax.rem(m + s, 8)], ens_r.at[m], ens_ss.at[s], ens_rs.at[s], at_mem(s)) for s in range(1, 8)
    ]
    for copy in ens_copies:
        copy.start()
    lax.fori_loop(EARLY, CHUNKS, with_copy, 0)

    rows_copy.wait_recv()
    for i in range(CHUNKS):
        flat_copy(i).wait_recv()
    ids = iota((256, OBD), 0).astype(F32)
    hot = jnp.concatenate(
        [jnp.where(ids == rows, 1.0, 0.0).astype(BF16), jnp.where(ids == rows_r[0:1], 1.0, 0.0).astype(BF16)], axis=1
    )

    def keep(r, sums):
        for q in range(4):
            s1[q, r] = sums[q * 32 : q * 32 + 32].astype(BF16)
        far1[0, r] = sums[128:136].astype(BF16)
        far1[1, r] = sums[136:144].astype(BF16)
        for k in range(7):
            acc1[k, r] = sums[144 + k * 16 : 160 + k * 16]

    def both_cores(r):
        return jnp.concatenate([flat_s[:, r].reshape(OBD, 128), flat_r[:, r].reshape(OBD, 128)], axis=0)

    def pair(k, carry):
        data = jnp.concatenate([both_cores(k * 2), both_cores(k * 2 + 1)], axis=1)
        sums = jnp.dot(hot, data, preferred_element_type=F32)
        for u in range(2):
            keep(k * 2 + u, sums[:, u * 128 : u * 128 + 128])
        return carry

    def copy1(q, g):
        span = pl.ds(*GROUPS[g])
        at = q * len(GROUPS) + g
        device = (at_y(1), at_y(3), at_x(1), at_x(3), at_y(2), at_x(2))[q]
        source, target = (s1.at[q, span], r1.at[q, span]) if q < 4 else (far1.at[q - 4, span], near1.at[q - 4, span])
        return remote(source, target, ss1.at[at], rs1.at[at], device)

    def copy2(q, g):
        span = pl.ds(*GROUPS[g])
        at = q * len(GROUPS) + g
        return remote(s2.at[q, span], r2.at[q, span], ss2.at[at], rs2.at[at], at_x(q + 1) if q < 3 else at_y(q - 2))

    def copy3(step, g):
        at = step * len(GROUPS) + g
        return remote(s3.at[step, g], r3.at[step, g], ss3.at[at], rs3.at[at], at_z(step))

    order = (4, 5, 0, 1, 2, 3)
    for g, (start, size) in enumerate(GROUPS):
        lax.fori_loop(start // 2, (start + size) // 2, pair, 0)
        if size % 2:
            keep(16, jnp.dot(hot, both_cores(16), preferred_element_type=F32))
        for q in order:
            copy1(q, g).start()

    for g, (start, size) in enumerate(GROUPS):
        span = pl.ds(start, size)
        def come(q, unit, span=span):
            return r1[q, span, unit * 16 : unit * 16 + 16].astype(F32)

        for q, source, unit in ((0, 0, 0), (3, 3, 0), (2, 1, 0), (5, 2, 0)):
            copy1(source, g).wait_recv()
            s2[q, span] = (acc1[q, span] + come(source, unit)).astype(BF16)
            copy2(q, g).start()
        for q in (4, 5):
            copy1(q, g).wait_recv()
        for axis, (q, one, two) in enumerate(((1, 0, 1), (4, 2, 3))):
            value = acc1[q, span] + come(one, 1) + come(two, 1)
            far = near1[axis, span].astype(F32)
            parts = [value[:, 0:8], value[:, 8:16]]
            parts[axis] = parts[axis] + far
            s2[q, span, 0:8] = parts[0].astype(BF16)
            s2[q, span, 8:16] = parts[1].astype(BF16)
            copy2(q, g).start()

    wide = acc2.reshape(2 * PACKED * 8, 128)

    def cell(half, step, start, size):
        return wide[pl.ds((half * PACKED + start) * 8 + step, size, stride=8), :]

    for g, (start, size) in enumerate(GROUPS):
        value = acc1[6, pl.ds(start, size)]
        for q in (0, 2, 3, 5, 1, 4):
            copy2(q, g).wait_recv()
            value = value + r2[q, pl.ds(start, size)].astype(F32)
        for half in range(2):
            acc2[pl.ds(half * PACKED + start, size)] = value[:, half * 8 : half * 8 + 8]
        for step in (4, 3, 5, 2, 6, 1, 7):
            for half in range(2):
                s3[step, g, half, 0:size] = cell(half, step, start, size).astype(BF16)
            copy3(step, g).start()

    for copy in ens_copies:
        copy.wait_recv()
    ens_r[m] = ens_s[m]
    for g in range(2):
        raw = ens_r[:, g].astype(F32).reshape(MEMBERS, 1024)
        mean = jnp.sum(raw, axis=0, keepdims=True) / MEMBERS
        means[g : g + 1] = mean
        pert_s[g * MEMBERS : g * MEMBERS + MEMBERS] = (raw - mean).astype(BF16)

    for g, (start, size) in enumerate(GROUPS):
        for step in (1, 7, 2, 6, 3, 5, 4):
            copy3(step, g).wait_recv()
        for half in range(2):
            value = cell(half, 0, start, size)
            for step in range(1, NZ):
                value = value + r3[step, g, half, 0:size].astype(F32)
            total[half, start : start + size] = value
    roots, projection = inverse_roots(total[0, 0:PACKED], total[1, 0:PACKED])

    spread = (jnp.sqrt(F32(MEMBERS - 1.0)) * roots).astype(BF16)
    result = jnp.dot(stacked(spread), pert_s[...], preferred_element_type=F32)
    for g in range(2):
        for k in range(8):
            at = g * MEMBERS + k * 8
            ana[k, g] = result[at : at + 8].astype(BF16)
    out_copies = [
        remote(ana.at[lax.rem(m + s, 8)], out_hbm.at[m], out_ss.at[s], out_rs.at[s], at_mem(s))
        for s in (4, 3, 5, 2, 6, 1, 7)
    ]
    for copy in out_copies:
        copy.start()
    mine = pltpu.make_async_copy(ana.at[m], out_hbm.at[m], own_sem.at[0])
    mine.start()

    weights = product(product(projection, roots), roots).astype(BF16)
    rise = jnp.dot(stacked(weights), pert_s[...], preferred_element_type=F32)
    mean_ref[...] = (means[0:2] + jnp.concatenate([rise[0:1], rise[8:9]], axis=0)).astype(BF16)
    mean_copy = pltpu.make_async_copy(mean_ref, mean_hbm, own_sem.at[1])
    mean_copy.start()

    for copy in ens_copies:
        copy.wait_send()
    rows_copy.wait_send()
    for i in range(CHUNKS):
        flat_copy(i).wait_send()
    for g in range(len(GROUPS)):
        for q in order:
            copy1(q, g).wait_send()
            copy2(q, g).wait_send()
        for step in range(1, NZ):
            copy3(step, g).wait_send()
    for copy in out_copies:
        copy.wait()
    mine.wait()
    mean_copy.wait()


def results(arrived_ref, mean_ref, out_hbm, mean_hbm, wide, turned, sem):
    copies = [pltpu.make_async_copy(mean_ref, mean_hbm, sem.at[8])]
    copies[0].start()
    for j in range(8):
        lanes = pl.ds(j * 128, 128)
        for g in range(16):
            wide[j, pl.ds(g, 8, stride=16), :] = arrived_ref[g, :, lanes].astype(F32)
        turned[:, :, lanes] = wide[j].reshape(8, 16, 128).astype(BF16)
        copies.append(pltpu.make_async_copy(turned.at[:, :, lanes], out_hbm.at[:, :, lanes], sem.at[j]))
        copies[-1].start()
    for copy in copies:
        copy.wait()


def body(ensemble, obs_members, obs_values, obs_weight, obs_count, obs_tile, obs_block, obs_turn):
    vmem, dma = pltpu.VMEM, pltpu.SemaphoreType.DMA
    whole = pl.BlockSpec(memory_space=pl.ANY)
    per = OBD // CHUNKS
    arrived, mean = pl.pallas_call(
        kernel,
        name="letkf",
        out_shape=(
            jax.ShapeDtypeStruct((8, 2, 8, 1024), BF16),
            jax.ShapeDtypeStruct((2, 1024), BF16),
        ),
        in_specs=[pl.BlockSpec(memory_space=pltpu.HBM)] * 8,
        out_specs=(whole, whole),
        scratch_shapes=[
            vmem((8, 16, 1024), BF16),
            vmem((OBD, ROWS), F32),
            vmem((OBD, ROWS), F32),
            vmem((1, OBD), jnp.int32),
            vmem((1, OBD), jnp.int32),
            vmem((1, OBD), jnp.int32),
            vmem((1, OBD), jnp.int32),
            vmem((2, 1024), BF16),
            vmem((OBD, MEMBERS, ROWS), BF16),
            vmem((8, 128, 128), F32),
            vmem((8, 2, 8, 1024), BF16),
            vmem((8, 2, 8, 1024), BF16),
            vmem((8, 1024), F32),
            vmem((2 * MEMBERS, 1024), BF16),
            vmem((OBD, ROWS), F32),
            vmem((PACKED * per, 128), F32),
            vmem((CHUNKS, PACKED, per, 128), BF16),
            vmem((CHUNKS, PACKED, per, 128), BF16),
            vmem((8, OBD), F32),
            vmem((8, OBD), F32),
            vmem((4, PACKED, 32, 128), BF16),
            vmem((4, PACKED, 32, 128), BF16),
            vmem((2, PACKED, 8, 128), BF16),
            vmem((2, PACKED, 8, 128), BF16),
            vmem((7, PACKED, 16, 128), F32),
            vmem((6, PACKED, 16, 128), BF16),
            vmem((6, PACKED, 16, 128), BF16),
            vmem((2 * PACKED, 8, 128), F32),
            vmem((NZ, len(GROUPS), 2, 8, 128), BF16),
            vmem((NZ, len(GROUPS), 2, 8, 128), BF16),
            vmem((2, 24, 128), F32),
            vmem((8, 2, 8, 1024), BF16),
            dma((CHUNKS,)), dma((7,)),
            dma((8,)), dma((8,)),
            dma((CHUNKS + 1,)), dma((CHUNKS + 1,)),
            dma((8 * len(GROUPS),)), dma((8 * len(GROUPS),)),
            dma((8 * len(GROUPS),)), dma((8 * len(GROUPS),)),
            dma((8 * len(GROUPS),)), dma((8 * len(GROUPS),)),
            dma((8,)), dma((8,)),
            dma((2,)),
        ],
        compiler_params=pltpu.CompilerParams(
            collective_id=0, has_side_effects=True, vmem_limit_bytes=48 << 20
        ),
    )(
        *(
            pltpu.with_memory_space_constraint(v, pltpu.HBM)
            for v in (
                ensemble,
                obs_members,
                obs_values,
                obs_weight,
                obs_count.reshape(1, OBD),
                obs_tile.reshape(1, OBD),
                obs_block.reshape(1, OBD),
                obs_turn.reshape(1, OBD),
            )
        )
    )
    return pl.pallas_call(
        results,
        name="results",
        out_shape=(
            jax.ShapeDtypeStruct((8, 16, 1024), BF16),
            jax.ShapeDtypeStruct((2, 1024), BF16),
        ),
        in_specs=[pl.BlockSpec(memory_space=pltpu.VMEM)] * 2,
        out_specs=(whole, whole),
        scratch_shapes=[vmem((8, 128, 128), F32), vmem((8, 16, 1024), BF16), dma((9,))],
        compiler_params=pltpu.CompilerParams(vmem_limit_bytes=16 << 20),
    )(arrived.reshape(16, 8, 1024), mean)


def solution(mesh):
    placed = (
        P("mem", "tile", None),
        P(("tile", "mem"), None, None),
        P(("tile", "mem"), None),
        P(("tile", "mem"), None),
        P(("tile", "mem")),
        P(("tile", "mem")),
        P(("tile", "mem")),
        P(("tile", "mem")),
    )
    return jax.shard_map(
        body,
        mesh=mesh,
        in_specs=placed,
        out_specs=(P("mem", "tile", None), P(("tile", "mem"), None)),
        check_vma=False,
    )
```
